256 devices in a mesh: tm: 32 (over x, z), phase: 8 (over y, core).
Axes of the slice: x: 4, y: 4, z: 8, core: 2. Of those that a mesh axis runs over, the one named last changes fastest.
Arguments:
- frames: bfloat16 [2, 4096, 1024], P(None, 'tm'), may hold values from -6 to 6
- frame_counts: int32 [2, 128], replicated, may hold values from 1 to 32, as said below
- w_query: bfloat16 [8, 1024, 1024], P('phase')
- w_key: bfloat16 [8, 1024, 1024], P('phase')
- w_value: bfloat16 [8, 1024, 1024], P('phase'), may hold values from -0.1875 to 0.1875
- w_out: bfloat16 [8, 1024, 1024], P('phase'), may hold values from -0.1875 to 0.1875
- conv_kernel: bfloat16 [8, 31, 1024], P('phase'), may hold values from -1 to 1
- w_point: bfloat16 [8, 1024, 1024], P('phase'), may hold values from -0.1875 to 0.1875
Outputs:
- layer_outputs: bfloat16 [8, 2, 4096, 1024], P('phase', None, 'tm')
The draws below stay inside these ranges and needn't reach their ends.
Inputs may be any that keep to these rules, and one draw needn't show every extreme that they name: `frame_counts`: A segment's valid frames are its first ones; the largest count 32 occurs in every draw.
All inputs are finite; a program needn't handle non-finite values.
Results may differ from the reference program's by a relative error of at most 0.034.
Values may be sent and summed in bfloat16 or wider, within the bound.
A program may use at most 64 MiB of HBM per device.

```python
import math
import jax
import jax.numpy as jnp
from jax import lax

D = 1024
HEADS = 16
SEG = 32
LC = 64
NMEM = 4
KW = 31
MICRO = 2
SPAN = 4096
NSEGS = 128
LAYERS = 8


def draw_frame_counts(key, part):
    shape = (MICRO, NSEGS)
    picker = jax.random.randint(jax.random.fold_in(key, 21), shape, 0, 4)
    shorter = jax.random.randint(jax.random.fold_in(key, 22), shape, 1, SEG + 1)
    return jnp.where(picker == 0, shorter, SEG).astype(jnp.int32)


def projection(key, salt):
    shape = (LAYERS, D, D)
    own_part = jax.random.normal(jax.random.fold_in(key, salt), shape, jnp.float32)
    values = own_part / jnp.sqrt(jnp.float32(D))
    return values


def draw_w_query(key, part):
    return projection(key, 32).astype(jnp.bfloat16)


def draw_w_key(key, part):
    return projection(key, 33).astype(jnp.bfloat16)


def block_scale(stream_key, dims, pieces, low, high):
    gain = 1.0
    for axis_at, blocks in pieces:
        draws = jax.random.uniform(jax.random.fold_in(jax.random.fold_in(stream_key, 6), axis_at), (blocks,), jnp.float32, low / len(pieces), high / len(pieces))
        gain = gain * jnp.repeat(jnp.exp(draws), dims[axis_at] // blocks).reshape((-1,) + (1,) * (len(dims) - 1 - axis_at))
    return gain


def bell_draw(own_key, shape, scale, reach, cuts=(), kind=jnp.bfloat16):
    factor_of = block_scale(own_key, shape, cuts, -0.22, 0.18) if cuts else 1.0
    drawn = jax.random.normal(own_key, shape, jnp.float32) * scale * factor_of
    return jnp.minimum(jnp.maximum(drawn, -reach), reach).astype(kind)


def setup_inputs(seed: int = 0) -> dict:
    streams_of = jax.random.split(jax.random.key(seed), 9)
    return {
        "frames": bell_draw(streams_of[0], (MICRO, SPAN, D), 1.0, 6.0, ((1, 32),)),
        "frame_counts": draw_frame_counts(jax.random.fold_in(streams_of[8], 71), 0),
        "w_query": draw_w_query(jax.random.fold_in(streams_of[8], 71), 0),
        "w_key": draw_w_key(jax.random.fold_in(streams_of[8], 71), 0),
        "w_value": bell_draw(streams_of[4], (LAYERS, D, D), D ** -0.5, 0.1875, ((0, 8),)),
        "w_out": bell_draw(streams_of[5], (LAYERS, D, D), D ** -0.5, 0.1875, ((0, 8),)),
        "conv_kernel": bell_draw(streams_of[6], (LAYERS, KW, D), KW ** -0.5, 1.0, ((0, 8),)),
        "w_point": bell_draw(streams_of[7], (LAYERS, D, D), D ** -0.5, 0.1875, ((0, 8),)),
    }


EPSILON = 1e-05

def layer_norm(values):
    center = values - lax.optimization_barrier(jnp.mean(values, axis=-1, keepdims=True))
    spread = lax.optimization_barrier(jnp.mean(center * center, axis=-1, keepdims=True))
    return center * lax.rsqrt(spread + EPSILON)

def attend(queries, key_rows, value_rows, allowed):
    segments, query_len, model_width = queries.shape
    head_dim = model_width // HEADS
    split_q = queries.astype(jnp.float32).reshape(segments, query_len, HEADS, head_dim)
    split_k = key_rows.astype(jnp.float32).reshape(segments, key_rows.shape[1], HEADS, head_dim)
    split_v = value_rows.astype(jnp.float32).reshape(segments, value_rows.shape[1], HEADS, head_dim)
    scores = jnp.einsum('sqhd,skhd->shqk', split_q, split_k) / math.sqrt(head_dim)
    scores = jnp.where(allowed[:, None, None, :], scores, -1e+30)
    top_score = lax.optimization_barrier(jnp.max(scores, axis=-1, keepdims=True))
    exponent = jnp.exp(scores - top_score)
    weights = (exponent / lax.optimization_barrier(jnp.sum(exponent, axis=-1, keepdims=True))).astype(jnp.bfloat16)
    context = jnp.einsum('shqk,skhd->sqhd', weights.astype(jnp.float32), split_v)
    return context.reshape(segments, query_len, model_width)

def windows(rows_all, segments):
    back_blocks = LC // SEG
    blocks = rows_all.reshape((segments + back_blocks, SEG) + rows_all.shape[1:])
    return jnp.concatenate([blocks[offset:offset + segments] for offset in range(back_blocks + 1)], axis=1)

def bank(rows_all, segments):
    return jnp.stack([rows_all[offset:offset + segments] for offset in range(NMEM)], axis=1)

def one_layer(layer_in, counts, valid, query_weight, key_weight, value_weight, out_weight, kernel, point_weight):
    total_frames, model_width = layer_in.shape
    segments = counts.shape[0]
    inputs = layer_in.astype(jnp.float32)
    normed = layer_norm(inputs).astype(jnp.bfloat16)
    queries = jnp.dot(normed, query_weight, preferred_element_type=jnp.float32).astype(jnp.bfloat16)
    key_rows = jnp.dot(normed, key_weight, preferred_element_type=jnp.float32).astype(jnp.bfloat16)
    value_rows = jnp.dot(normed, value_weight, preferred_element_type=jnp.float32).astype(jnp.bfloat16)
    seg_mask = valid.reshape(segments, SEG)
    seg_rows = normed.reshape(segments, SEG, model_width).astype(jnp.float32)
    summary = (lax.optimization_barrier(jnp.sum(seg_rows * seg_mask[:, :, None], axis=1)) / counts[:, None].astype(jnp.float32)).astype(jnp.bfloat16)
    summary_q = jnp.dot(summary, query_weight, preferred_element_type=jnp.float32).astype(jnp.bfloat16)
    lead_rows = jnp.zeros((LC, model_width), jnp.bfloat16)
    key_win = windows(jnp.concatenate([lead_rows, key_rows]), segments)
    value_win = windows(jnp.concatenate([lead_rows, value_rows]), segments)
    mask_win = windows(jnp.concatenate([jnp.zeros((LC,), jnp.float32), valid]), segments) > 0.5
    memory = attend(summary_q[:, None, :], key_win, value_win, mask_win)[:, 0, :].astype(jnp.bfloat16)
    mem_k = jnp.dot(memory, key_weight, preferred_element_type=jnp.float32).astype(jnp.bfloat16)
    mem_v = jnp.dot(memory, value_weight, preferred_element_type=jnp.float32).astype(jnp.bfloat16)
    lead_mem = jnp.zeros((NMEM, model_width), jnp.bfloat16)
    bank_k = bank(jnp.concatenate([lead_mem, mem_k]), segments)
    bank_v = bank(jnp.concatenate([lead_mem, mem_v]), segments)
    bank_ok = bank(jnp.concatenate([jnp.zeros((NMEM,), jnp.int32), counts]), segments) > 0
    all_keys = jnp.concatenate([bank_k, key_win], axis=1)
    all_values = jnp.concatenate([bank_v, value_win], axis=1)
    all_ok = jnp.concatenate([bank_ok, mask_win], axis=1)
    context = attend(queries.reshape(segments, SEG, model_width), all_keys, all_values, all_ok)
    context = context.reshape(total_frames, model_width).astype(jnp.bfloat16)
    residual = (inputs + jnp.dot(context, out_weight, preferred_element_type=jnp.float32)).astype(jnp.bfloat16)
    conv_in = (layer_norm(residual.astype(jnp.float32)) * valid[:, None]).astype(jnp.bfloat16)
    extended = jnp.concatenate([jnp.zeros((KW - 1, model_width), jnp.bfloat16), conv_in])
    depth = jnp.zeros((total_frames, model_width), jnp.float32)
    for offset in range(KW):
        depth = depth + kernel[offset].astype(jnp.float32) * extended[offset:offset + total_frames].astype(jnp.float32)
    gated = jax.nn.silu(layer_norm(depth)).astype(jnp.bfloat16)
    mixed = residual.astype(jnp.float32) + jnp.dot(gated, point_weight, preferred_element_type=jnp.float32)
    return (mixed * valid[:, None]).astype(jnp.bfloat16)

def reference(frames, frame_counts, w_query, w_key, w_value, w_out, conv_kernel, w_point):
    micro_count, span_rows, model_width = frames.shape
    counts = frame_counts.reshape(-1).astype(jnp.int32)
    valid = (jnp.arange(SEG, dtype=jnp.int32)[None, :] < counts[:, None]).astype(jnp.float32).reshape(-1)
    hidden = frames.reshape(micro_count * span_rows, model_width)
    results = []
    for layer in range(LAYERS):
        hidden = one_layer(hidden, counts, valid, w_query[layer], w_key[layer], w_value[layer], w_out[layer], conv_kernel[layer], w_point[layer])
        results.append(hidden.reshape(micro_count, span_rows, model_width))
    return jnp.stack(results)
```

```python
import functools

import jax
import jax.numpy as jnp
from jax import lax
from jax.experimental import pallas as pl
from jax.experimental.pallas import tpu as pltpu
from jax.sharding import PartitionSpec as P

HEADS = 16
SEG = 32
LC = 64
NMEM = 4
KW = 31
EPS = 1e-05
NEG = -1e30
F32 = jnp.float32
BF16 = jnp.bfloat16
MESH = pl.DeviceIdType.MESH


def layer_norm(v):
    width = v.shape[-1]
    c = v - jnp.sum(v, axis=-1, keepdims=True) * (1.0 / width)
    s = jnp.sum(c * c, axis=-1, keepdims=True) * (1.0 / width)
    return c * lax.rsqrt(s + EPS)


def dot_nt(a, b):
    return lax.dot_general(a, b, (((1,), (1,)), ((), ())), preferred_element_type=F32)


def dot_nn(a, b):
    return jnp.dot(a, b, preferred_element_type=F32)


def relay_kernel(
    shards, phases, micro, rows, width,
    counts, frames, w_query, w_key, w_value, w_out, w_conv, w_point,
    out,
    wq, wk, wv, wo, wc, wp,
    xin, nbuf, kbuf, vbuf, qbuf, cbuf, rbuf, cext, dbuf, gbuf, obuf, taps,
    mem_out, mem_in, memk, memv, rim_out, rim_in,
    w_sem, fr_sem, out_sem,
    x_send, x_recv, xh_send, xh_recv, mem_send, mem_recv, rim_send, rim_recv,
):
    t = lax.axis_index("tm")
    p = lax.axis_index("phase")
    segs = rows // SEG
    span_segs = shards * segs
    t_next = lax.rem(t + 1, shards)
    t_prev = lax.rem(t + shards - 1, shards)
    p_next = lax.rem(p + 1, phases)
    p_prev = lax.rem(p + phases - 1, phases)
    first_phase = p == 0
    has_next = p < phases - 1
    last_shard = t == shards - 1
    wrap = jnp.where(last_shard, 1, 0)

    loads = [
        pltpu.make_async_copy(src.at[0], dst, w_sem.at[i])
        for i, (src, dst) in enumerate(
            [(w_key, wk), (w_value, wv), (w_query, wq), (w_out, wo), (w_conv, wc), (w_point, wp)]
        )
    ]

    def frame_load(m):
        return pltpu.make_async_copy(frames.at[m], xin.at[m, pl.ds(LC, rows)], fr_sem.at[m])

    @pl.when(first_phase)
    def _():
        for m in range(micro):
            frame_load(m).start()

    for load in loads:
        load.start()

    barrier = pltpu.get_barrier_semaphore()
    for dt, dp in (
        (t_next, p), (t_prev, p), (t, p_next), (t, p_prev), (t_next, p_next), (t_prev, p_prev)
    ):
        pl.semaphore_signal(barrier, inc=1, device_id=(dt, dp), device_id_type=MESH)
    pl.semaphore_wait(barrier, 6)

    def sends_right(m):
        return jnp.logical_or(t < shards - 1, m < micro - 1)

    def has_left(m):
        return jnp.logical_or(t > 0, m > 0)

    def first_halo(m):
        slot = jnp.minimum(m + wrap, micro - 1)
        return pltpu.make_async_remote_copy(
            src_ref=frames.at[m, pl.ds(rows - LC, LC)],
            dst_ref=xin.at[slot, pl.ds(0, LC)],
            send_sem=xh_send.at[micro + m], recv_sem=xh_recv.at[slot],
            device_id=(t_next, p), device_id_type=MESH,
        )

    def block_send(m):
        return pltpu.make_async_remote_copy(
            src_ref=obuf.at[m],
            dst_ref=xin.at[m, pl.ds(LC, rows)],
            send_sem=x_send.at[m], recv_sem=x_recv.at[m],
            device_id=(t, p_next), device_id_type=MESH,
        )

    def to_slot(m):
        return jnp.minimum(m + wrap, micro - 1)

    def halo_send(m, slot):
        return pltpu.make_async_remote_copy(
            src_ref=obuf.at[m, pl.ds(rows - LC, LC)],
            dst_ref=xin.at[slot, pl.ds(0, LC)],
            send_sem=xh_send.at[m], recv_sem=xh_recv.at[slot],
            device_id=(t_next, p_next), device_id_type=MESH,
        )

    def mem_copy(m, slot):
        return pltpu.make_async_remote_copy(
            src_ref=mem_out.at[m], dst_ref=mem_in.at[slot],
            send_sem=mem_send.at[m], recv_sem=mem_recv.at[slot],
            device_id=(t_next, p), device_id_type=MESH,
        )

    def rim_copy(m, slot):
        return pltpu.make_async_remote_copy(
            src_ref=rim_out.at[m], dst_ref=rim_in.at[slot],
            send_sem=rim_send.at[m], recv_sem=rim_recv.at[slot],
            device_id=(t_next, p), device_id_type=MESH,
        )

    def out_copy(m):
        return pltpu.make_async_copy(obuf.at[m], out.at[0, m], out_sem.at[m])

    @pl.when(first_phase)
    def _():
        for m in range(micro):
            @pl.when(sends_right(m))
            def _():
                first_halo(m).start()

    @pl.when(t == 0)
    def _():
        xin[0, 0:LC, :] = jnp.zeros((LC, width), BF16)
        mem_in[0] = jnp.zeros(mem_in.shape[1:], F32)
        rim_in[0] = jnp.zeros(rim_in.shape[1:], BF16)

    loads[4].wait()
    for j in range(KW):
        taps[j] = jnp.broadcast_to(wc[j : j + 1, :].astype(F32), (8, width))

    def count_of(m, rel):
        s = m * span_segs + t * segs + rel
        safe = jnp.maximum(s, 0)
        value = counts[safe // span_segs, lax.rem(safe, span_segs)]
        return jnp.where(s >= 0, value, 0)

    def one_block(m, carry):
        near = [count_of(m, rel) for rel in range(-segs, segs)]
        left = LC // SEG

        @pl.when(first_phase)
        def _():
            frame_load(m).wait()

        @pl.when(jnp.logical_not(first_phase))
        def _():
            block_send(m).wait_recv()

        @pl.when(has_left(m))
        def _():
            halo_send(m, m).wait_recv()

        total = LC + rows

        def norm_rows(i, c):
            r = pl.multiple_of(i * 16, 16)
            nbuf[pl.ds(r, 16), :] = layer_norm(xin[m, pl.ds(r, 16), :].astype(F32)).astype(BF16)
            return c

        lax.fori_loop(0, total // 16, norm_rows, 0, unroll=4)

        srow = lax.broadcasted_iota(jnp.int32, (16, rows), 0)
        scol = lax.broadcasted_iota(jnp.int32, (16, rows), 1)
        cnt_lane = jnp.zeros((16, rows), jnp.int32)
        cnt_col = jnp.ones((16, 1), jnp.int32)
        crow = lax.broadcasted_iota(jnp.int32, (16, 1), 0)
        for i in range(segs):
            cnt_lane = jnp.where(scol // SEG == i, near[segs + i], cnt_lane)
            cnt_col = jnp.where(crow == i, near[segs + i], cnt_col)
        pick = jnp.logical_and(srow == scol // SEG, lax.rem(scol, SEG) < cnt_lane)
        pick = jnp.where(pick, 1.0, 0.0).astype(BF16)
        summary = dot_nn(pick, nbuf[LC:total, :]) / cnt_col.astype(F32)
        nbuf[total : total + 16, :] = summary.astype(BF16)

        @pl.when(m == 0)
        def _():
            for i in (0, 1, 2):
                loads[i].wait()

        def project(n, c):
            col = pl.ds(pl.multiple_of(n * 256, 256), 256)
            kbuf[:, col] = dot_nn(nbuf[0:total, :], wk[:, col]).astype(BF16)
            vbuf[:, col] = dot_nn(nbuf[0:total, :], wv[:, col]).astype(BF16)
            qbuf[:, col] = (dot_nn(nbuf[LC : total + 16, :], wq[:, col]).astype(BF16).astype(F32) * 0.125).astype(BF16)
            return c

        lax.fori_loop(0, width // 256, project, 0)

        nq = segs * HEADS
        hrow = lax.broadcasted_iota(jnp.int32, (HEADS, width), 0)
        hcol = lax.broadcasted_iota(jnp.int32, (HEADS, width), 1) // (width // HEADS)
        head_on = hrow == hcol
        sq = qbuf[rows : rows + 16, :].astype(F32)
        queries = jnp.concatenate(
            [
                jnp.where(head_on, jnp.broadcast_to(sq[i : i + 1, :], (HEADS, width)), 0.0)
                for i in range(segs)
            ],
            axis=0,
        ).astype(BF16)
        mrow = lax.broadcasted_iota(jnp.int32, (nq, total), 0) // HEADS
        mcol = lax.broadcasted_iota(jnp.int32, (nq, total), 1)
        mseg = mcol // SEG
        cnt_key = jnp.zeros((nq, total), jnp.int32)
        for i in range(left + segs):
            cnt_key = jnp.where(mseg == i, near[segs - left + i], cnt_key)
        ok = (mseg >= mrow) & (mseg <= mrow + left) & (lax.rem(mcol, SEG) < cnt_key)
        scores = jnp.where(ok, dot_nt(queries, kbuf[...]), NEG)
        expo = jnp.exp(scores - jnp.max(scores, axis=-1, keepdims=True))
        weights = (expo / jnp.sum(expo, axis=-1, keepdims=True)).astype(BF16)
        mixed = dot_nn(weights, vbuf[...])
        memory = jnp.concatenate(
            [
                jnp.sum(jnp.where(head_on, mixed[i * HEADS : (i + 1) * HEADS, :], 0.0), axis=0, keepdims=True)
                for i in range(segs)
            ]
            + [jnp.zeros((16 - segs, width), F32)],
            axis=0,
        ).astype(BF16)
        gbuf[0:16, :] = memory

        def mem_project(n, c):
            col = pl.ds(pl.multiple_of(n * 256, 256), 256)
            mk = dot_nn(gbuf[0:16, :], wk[:, col]).astype(BF16).astype(F32)
            mv = dot_nn(gbuf[0:16, :], wv[:, col]).astype(BF16).astype(F32)
            mem_out[m, 0:NMEM, col] = mk[0:NMEM]
            mem_out[m, NMEM : 2 * NMEM, col] = mv[0:NMEM]
            return c

        lax.fori_loop(0, width // 256, mem_project, 0)

        @pl.when(sends_right(m))
        def _():
            mem_copy(m, to_slot(m)).start()

        @pl.when(has_left(m))
        def _():
            mem_copy(m, m).wait_recv()

        pad = jnp.zeros((SEG - 2 * NMEM, width), F32)
        memk[...] = jnp.concatenate([mem_in[m, 0:NMEM, :], mem_out[m, 0:NMEM, :], pad], axis=0).astype(BF16)
        memv[...] = jnp.concatenate(
            [mem_in[m, NMEM : 2 * NMEM, :], mem_out[m, NMEM : 2 * NMEM, :], pad], axis=0
        ).astype(BF16)

        quad = 4
        qw = quad * (width // HEADS)
        win = LC + SEG
        lane = lax.broadcasted_iota(jnp.int32, (1, 128), 1)
        lane_seg = lane // SEG
        biases = []
        for i in range(segs):
            cnt = jnp.zeros((1, 128), jnp.int32)
            for j in range(left + 1):
                cnt = jnp.where(lane_seg == j, near[segs - left + i + j], cnt)
            okay = (lane < win) & (lax.rem(lane, SEG) < cnt)
            for j in range(NMEM):
                okay = okay | ((lane == win + i + j) & (near[i + j] > 0))
            biases.append(jnp.where(okay, 0.0, NEG))
        qlane = lax.broadcasted_iota(jnp.int32, (1, qw), 1) // (width // HEADS)
        sel = [jnp.where(qlane == h, 1.0, 0.0).astype(BF16) for h in range(quad)]

        def attend(g, c):
            col = pl.ds(pl.multiple_of(g * qw, qw), qw)
            mk = memk[:, col]
            mv = memv[:, col]
            for i in range(segs):
                q = qbuf[i * SEG : (i + 1) * SEG, col]
                q4 = jnp.concatenate([q * sel[h] for h in range(quad)], axis=0)
                ks = jnp.concatenate([kbuf[i * SEG : i * SEG + win, col], mk], axis=0)
                vs = jnp.concatenate([vbuf[i * SEG : i * SEG + win, col], mv], axis=0)
                s = dot_nt(q4, ks) + biases[i]
                e = jnp.exp(s - jnp.max(s, axis=-1, keepdims=True))
                o = dot_nn(e.astype(BF16), vs) / jnp.sum(e, axis=-1, keepdims=True)
                ctx = jnp.where(qlane == 0, o[0:SEG], 0.0)
                for h in range(1, quad):
                    ctx = jnp.where(qlane == h, o[h * SEG : (h + 1) * SEG], ctx)
                cbuf[i * SEG : (i + 1) * SEG, col] = ctx.astype(BF16)
            return c

        lax.fori_loop(0, width // qw, attend, 0)

        @pl.when(m == 0)
        def _():
            loads[3].wait()

        def project_out(n, c):
            col = pl.ds(pl.multiple_of(n * 256, 256), 256)
            r = xin[m, LC:total, col].astype(F32) + dot_nn(cbuf[...], wo[:, col])
            rbuf[:, col] = r.astype(BF16)
            return c

        lax.fori_loop(0, width // 256, project_out, 0)

        def row_mask(i):
            seg = i // 2
            cnt = count_of(m, seg)
            ids = lax.broadcasted_iota(jnp.int32, (16, 1), 0) + lax.rem(i, 2) * 16
            return jnp.where(ids < cnt, 1.0, 0.0)

        def conv_rows(i, c):
            r = pl.multiple_of(i * 16, 16)
            z = (layer_norm(rbuf[pl.ds(r, 16), :].astype(F32)) * row_mask(i)).astype(BF16)
            cext[pl.ds(r + SEG, 16), :] = z.astype(F32)
            return c

        lax.fori_loop(0, rows // 16, conv_rows, 0, unroll=4)
        rim_out[m] = cext[rows : rows + SEG, :].astype(BF16)

        @pl.when(sends_right(m))
        def _():
            rim_copy(m, to_slot(m)).start()

        sub = lax.broadcasted_iota(jnp.int32, (8, 128), 0)

        def conv_range(k0, k1):
            def body(cb, c):
                col = pl.ds(pl.multiple_of(cb * 128, 128), 128)
                a = {}

                def get(k):
                    if k not in a:
                        a[k] = cext[8 * k : 8 * k + 8, col]
                    return a[k]

                def tap(o):
                    return taps[o - 2, :, col]

                acc = {}
                for s in range(8):
                    offs = [o for o in range(s, KW + 2, 8) if 2 <= o <= KW + 1]
                    prev = None
                    for k in range(k0, k1 + (1 if s else 0)):
                        y = None
                        for o in offs:
                            term = tap(o) * get(k + o // 8)
                            y = term if y is None else y + term
                        if s == 0:
                            acc[k] = y
                            continue
                        y = pltpu.roll(y, 8 - s, axis=0)
                        if prev is not None:
                            acc[k - 1] = acc[k - 1] + jnp.where(sub < 8 - s, prev, y)
                        prev = y
                for k in range(k0, k1):
                    dbuf[8 * k : 8 * k + 8, col] = acc[k]
                return c

            lax.fori_loop(0, width // 128, body, 0)

        conv_range(SEG // 8, rows // 8)

        @pl.when(has_left(m))
        def _():
            rim_copy(m, m).wait_recv()

        cext[0:SEG, :] = rim_in[m].astype(F32)
        conv_range(0, SEG // 8)

        def gate_rows(i, c):
            r = pl.multiple_of(i * 16, 16)
            z = layer_norm(dbuf[pl.ds(r, 16), :])
            gbuf[pl.ds(r, 16), :] = (z / (1.0 + jnp.exp(-z))).astype(BF16)
            return c

        lax.fori_loop(0, rows // 16, gate_rows, 0, unroll=4)

        @pl.when(m == 0)
        def _():
            loads[5].wait()

        vrow = lax.broadcasted_iota(jnp.int32, (rows, 1), 0)
        cnt_row = jnp.zeros((rows, 1), jnp.int32)
        for i in range(segs):
            cnt_row = jnp.where(vrow // SEG == i, near[segs + i], cnt_row)
        keep = jnp.where(lax.rem(vrow, SEG) < cnt_row, 1.0, 0.0)

        def project_point(n, c):
            col = pl.ds(pl.multiple_of(n * 256, 256), 256)
            y = rbuf[:, col].astype(F32) + dot_nn(gbuf[...], wp[:, col])
            obuf[m, :, col] = (y * keep).astype(BF16)
            return c

        lax.fori_loop(0, width // 256, project_point, 0)

        @pl.when(has_next)
        def _():
            block_send(m).start()

            @pl.when(sends_right(m))
            def _():
                halo_send(m, to_slot(m)).start()

        out_copy(m).start()
        return carry

    lax.fori_loop(0, micro, one_block, 0)

    for m in range(micro):
        out_copy(m).wait()

        @pl.when(has_next)
        def _():
            block_send(m).wait_send()

        @pl.when(sends_right(m))
        def _():
            mem_copy(m, to_slot(m)).wait_send()
            rim_copy(m, to_slot(m)).wait_send()

            @pl.when(has_next)
            def _():
                halo_send(m, to_slot(m)).wait_send()

            @pl.when(first_phase)
            def _():
                first_halo(m).wait_send()


def per_device(frames, frame_counts, w_query, w_key, w_value, w_out, conv_kernel, w_point):
    micro, rows, width = frames.shape
    shards = lax.axis_size("tm")
    phases = lax.axis_size("phase")
    dma = pltpu.SemaphoreType.DMA
    any_spec = pl.BlockSpec(memory_space=pl.ANY)
    mat = pltpu.VMEM((width, width), BF16)
    return pl.pallas_call(
        functools.partial(relay_kernel, shards, phases, micro, rows, width),
        out_shape=jax.ShapeDtypeStruct((1, micro, rows, width), BF16),
        in_specs=[pl.BlockSpec(memory_space=pltpu.SMEM)] + [any_spec] * 7,
        out_specs=any_spec,
        scratch_shapes=[
            mat, mat, mat, mat, pltpu.VMEM((KW, width), BF16), mat,
            pltpu.VMEM((micro, LC + rows, width), BF16),
            pltpu.VMEM((LC + rows + 16, width), BF16),
            pltpu.VMEM((LC + rows, width), BF16),
            pltpu.VMEM((LC + rows, width), BF16),
            pltpu.VMEM((rows + 16, width), BF16),
            pltpu.VMEM((rows, width), BF16),
            pltpu.VMEM((rows, width), BF16),
            pltpu.VMEM((SEG + rows, width), F32),
            pltpu.VMEM((rows, width), F32),
            pltpu.VMEM((rows, width), BF16),
            pltpu.VMEM((micro, rows, width), BF16),
            pltpu.VMEM((KW, 8, width), F32),
            pltpu.VMEM((micro, 2 * NMEM, width), F32),
            pltpu.VMEM((micro, 2 * NMEM, width), F32),
            pltpu.VMEM((SEG, width), BF16),
            pltpu.VMEM((SEG, width), BF16),
            pltpu.VMEM((micro, SEG, width), BF16),
            pltpu.VMEM((micro, SEG, width), BF16),
            dma((6,)), dma((micro,)), dma((micro,)),
            dma((micro,)), dma((micro,)), dma((2 * micro,)), dma((micro,)),
            dma((micro,)), dma((micro,)), dma((micro,)), dma((micro,)),
        ],
        compiler_params=pltpu.CompilerParams(
            collective_id=0, has_side_effects=True, vmem_limit_bytes=48 * 1024 * 1024
        ),
    )(frame_counts, frames, w_query, w_key, w_value, w_out, conv_kernel, w_point)


def solution(mesh):
    stage = P("phase", None, None)
    return jax.shard_map(
        per_device,
        mesh=mesh,
        in_specs=(P(None, "tm", None), P(), stage, stage, stage, stage, stage, stage),
        out_specs=P("phase", None, "tm", None),
        check_vma=False,
    )
```

```python
import functools

import jax
import jax.numpy as jnp
from jax import lax
from jax.experimental import pallas as pl
from jax.experimental.pallas import tpu as pltpu
from jax.sharding import PartitionSpec as P

HEADS = 16
SEG = 32
LC = 64
NMEM = 4
KW = 31
EPS = 1e-05
NEG = -1e30
PIECES = ((32, 128), (0, 32))
F32 = jnp.float32
BF16 = jnp.bfloat16
MESH = pl.DeviceIdType.MESH


def layer_norm(v):
    width = v.shape[-1]
    c = v - jnp.sum(v, axis=-1, keepdims=True) * (1.0 / width)
    s = jnp.sum(c * c, axis=-1, keepdims=True) * (1.0 / width)
    return c * lax.rsqrt(s + EPS)


def dot_nt(a, b):
    return lax.dot_general(a, b, (((1,), (1,)), ((), ())), preferred_element_type=F32)


def dot_nn(a, b):
    return jnp.dot(a, b, preferred_element_type=F32)


def relay_kernel(
    shards, phases, micro, rows, width,
    counts, frames, w_query, w_key, w_value, w_out, w_conv, w_point,
    out,
    wq, wk, wv, wo, wc, wp,
    xin, nbuf, kbuf, vbuf, qbuf, cbuf, rbuf, cext, dbuf, gbuf, obuf, taps,
    mem_out, mem_in, memk, memv, rim_out, rim_in,
    w_sem, fr_sem, out_sem,
    x_send, x_recv, xh_send, xh_recv, mem_send, mem_recv, rim_send, rim_recv,
):
    t = lax.axis_index("tm")
    p = lax.axis_index("phase")
    segs = rows // SEG
    span_segs = shards * segs
    t_next = lax.rem(t + 1, shards)
    t_prev = lax.rem(t + shards - 1, shards)
    p_next = lax.rem(p + 1, phases)
    p_prev = lax.rem(p + phases - 1, phases)
    first_phase = p == 0
    has_next = p < phases - 1
    last_shard = t == shards - 1
    wrap = jnp.where(last_shard, 1, 0)

    loads = [
        pltpu.make_async_copy(src.at[0], dst, w_sem.at[i])
        for i, (src, dst) in enumerate(
            [(w_key, wk), (w_value, wv), (w_query, wq), (w_out, wo), (w_conv, wc), (w_point, wp)]
        )
    ]

    def frame_load(m):
        return pltpu.make_async_copy(frames.at[m], xin.at[m, pl.ds(LC, rows)], fr_sem.at[m])

    @pl.when(first_phase)
    def _():
        for m in range(micro):
            frame_load(m).start()

    for load in loads:
        load.start()

    barrier = pltpu.get_barrier_semaphore()
    for dt, dp in (
        (t_next, p), (t_prev, p), (t, p_next), (t, p_prev), (t_next, p_next), (t_prev, p_prev)
    ):
        pl.semaphore_signal(barrier, inc=1, device_id=(dt, dp), device_id_type=MESH)
    pl.semaphore_wait(barrier, 6)

    def sends_right(m):
        return jnp.logical_or(t < shards - 1, m < micro - 1)

    def has_left(m):
        return jnp.logical_or(t > 0, m > 0)

    def first_halo(m):
        slot = jnp.minimum(m + wrap, micro - 1)
        return pltpu.make_async_remote_copy(
            src_ref=frames.at[m, pl.ds(rows - LC, LC)],
            dst_ref=xin.at[slot, pl.ds(0, LC)],
            send_sem=xh_send.at[micro + m], recv_sem=xh_recv.at[slot],
            device_id=(t_next, p), device_id_type=MESH,
        )

    def piece_send(m, n):
        lo, hi = PIECES[n]
        return pltpu.make_async_remote_copy(
            src_ref=obuf.at[m, pl.ds(lo, hi - lo)],
            dst_ref=xin.at[m, pl.ds(LC + lo, hi - lo)],
            send_sem=x_send.at[m, n], recv_sem=x_recv.at[m, n],
            device_id=(t, p_next), device_id_type=MESH,
        )

    def to_slot(m):
        return jnp.minimum(m + wrap, micro - 1)

    def halo_send(m, slot):
        return pltpu.make_async_remote_copy(
            src_ref=obuf.at[m, pl.ds(rows - LC, LC)],
            dst_ref=xin.at[slot, pl.ds(0, LC)],
            send_sem=xh_send.at[m], recv_sem=xh_recv.at[slot],
            device_id=(t_next, p_next), device_id_type=MESH,
        )

    def mem_copy(m, slot):
        return pltpu.make_async_remote_copy(
            src_ref=mem_out.at[m], dst_ref=mem_in.at[slot],
            send_sem=mem_send.at[m], recv_sem=mem_recv.at[slot],
            device_id=(t_next, p), device_id_type=MESH,
        )

    def rim_copy(m, slot):
        return pltpu.make_async_remote_copy(
            src_ref=rim_out.at[m], dst_ref=rim_in.at[slot],
            send_sem=rim_send.at[m], recv_sem=rim_recv.at[slot],
            device_id=(t_next, p), device_id_type=MESH,
        )

    def out_copy(m):
        return pltpu.make_async_copy(obuf.at[m], out.at[0, m], out_sem.at[m])

    @pl.when(first_phase)
    def _():
        for m in range(micro):
            @pl.when(sends_right(m))
            def _():
                first_halo(m).start()

    @pl.when(t == 0)
    def _():
        xin[0, 0:LC, :] = jnp.zeros((LC, width), BF16)
        mem_in[0] = jnp.zeros(mem_in.shape[1:], BF16)
        rim_in[0] = jnp.zeros(rim_in.shape[1:], BF16)

    memk[...] = jnp.zeros(memk.shape, F32)
    memv[...] = jnp.zeros(memv.shape, F32)
    loads[4].wait()
    for j in range(KW):
        taps[j] = jnp.broadcast_to(wc[j : j + 1, :].astype(F32), (8, width))

    def count_of(m, rel):
        s = m * span_segs + t * segs + rel
        safe = jnp.maximum(s, 0)
        value = counts[safe // span_segs, lax.rem(safe, span_segs)]
        return jnp.where(s >= 0, value, 0)

    def one_block(m, carry):
        near = [count_of(m, rel) for rel in range(-segs, segs)]
        left = LC // SEG

        total = LC + rows

        def norm_rows(lo, hi):
            for r in range(lo, hi, 16):
                nbuf[r : r + 16, :] = layer_norm(xin[m, r : r + 16, :].astype(F32)).astype(BF16)

        @pl.when(first_phase)
        def _():
            frame_load(m).wait()

        def wait_piece(n):
            @pl.when(jnp.logical_not(first_phase))
            def _():
                piece_send(m, n).wait_recv()

        wait_piece(0)

        def sec_norm2():
            norm_rows(LC + PIECES[0][0], LC + PIECES[0][1])

        sec_norm2()

        @pl.when(has_left(m))
        def _():
            halo_send(m, m).wait_recv()

        def sec_normh():
            norm_rows(0, LC)

        sec_normh()
        wait_piece(1)

        def sec_norm1():
            norm_rows(LC + PIECES[1][0], LC + PIECES[1][1])

        sec_norm1()

        def sec_summary():
            srow = lax.broadcasted_iota(jnp.int32, (16, rows), 0)
            scol = lax.broadcasted_iota(jnp.int32, (16, rows), 1)
            cnt_lane = jnp.zeros((16, rows), jnp.int32)
            cnt_col = jnp.ones((16, 1), jnp.int32)
            crow = lax.broadcasted_iota(jnp.int32, (16, 1), 0)
            for i in range(segs):
                cnt_lane = jnp.where(scol // SEG == i, near[segs + i], cnt_lane)
                cnt_col = jnp.where(crow == i, near[segs + i], cnt_col)
            pick = jnp.logical_and(srow == scol // SEG, lax.rem(scol, SEG) < cnt_lane)
            pick = jnp.where(pick, 1.0, 0.0).astype(BF16)
            summary = dot_nn(pick, nbuf[LC:total, :]) / cnt_col.astype(F32)
            nbuf[total : total + 16, :] = summary.astype(BF16)

        sec_summary()

        @pl.when(m == 0)
        def _():
            for i in (0, 1, 2):
                loads[i].wait()

        def sec_project():
            def project(n, c):
                col = pl.ds(pl.multiple_of(n * 256, 256), 256)
                kbuf[:, col] = dot_nn(nbuf[0:total, :], wk[:, col]).astype(BF16)
                vbuf[:, col] = dot_nn(nbuf[0:total, :], wv[:, col]).astype(BF16)
                qbuf[:, col] = (dot_nn(nbuf[LC : total + 16, :], wq[:, col]).astype(BF16).astype(F32) * 0.125).astype(BF16)
                return c

            lax.fori_loop(0, width // 256, project, 0, unroll=True)

        sec_project()

        def sec_memory():
            nq = segs * HEADS
            hrow = lax.broadcasted_iota(jnp.int32, (HEADS, width), 0)
            hcol = lax.broadcasted_iota(jnp.int32, (HEADS, width), 1) // (width // HEADS)
            head_on = hrow == hcol
            sq = qbuf[rows : rows + 16, :].astype(F32)
            queries = jnp.concatenate(
                [
                    jnp.where(head_on, jnp.broadcast_to(sq[i : i + 1, :], (HEADS, width)), 0.0)
                    for i in range(segs)
                ],
                axis=0,
            ).astype(BF16)
            mrow = lax.broadcasted_iota(jnp.int32, (nq, total), 0) // HEADS
            mcol = lax.broadcasted_iota(jnp.int32, (nq, total), 1)
            mseg = mcol // SEG
            cnt_key = jnp.zeros((nq, total), jnp.int32)
            for i in range(left + segs):
                cnt_key = jnp.where(mseg == i, near[segs - left + i], cnt_key)
            ok = (mseg >= mrow) & (mseg <= mrow + left) & (lax.rem(mcol, SEG) < cnt_key)
            scores = jnp.where(ok, dot_nt(queries, kbuf[...]), NEG)
            expo = jnp.exp(scores - jnp.max(scores, axis=-1, keepdims=True))
            weights = (expo / jnp.sum(expo, axis=-1, keepdims=True)).astype(BF16)
            mixed = dot_nn(weights, vbuf[...])
            memory = jnp.concatenate(
                [
                    jnp.sum(jnp.where(head_on, mixed[i * HEADS : (i + 1) * HEADS, :], 0.0), axis=0, keepdims=True)
                    for i in range(segs)
                ]
                * 4,
                axis=0,
            ).astype(BF16)
            gbuf[0:16, :] = memory

        sec_memory()

        def sec_memproj():
            low = lax.broadcasted_iota(jnp.int32, (2 * NMEM, 256), 0) < NMEM

            def mem_project(n, c):
                col = pl.ds(pl.multiple_of(n * 256, 256), 256)
                mk = dot_nn(gbuf[0:16, :], wk[:, col])[0 : 2 * NMEM]
                mv = dot_nn(gbuf[0:16, :], wv[:, col])[0 : 2 * NMEM]
                mem_out[m, :, col] = jnp.where(low, mk, mv).astype(BF16)
                memk[0 : 2 * NMEM, col] = mk
                memv[0 : 2 * NMEM, col] = mv
                return c

            lax.fori_loop(0, width // 256, mem_project, 0, unroll=True)

        sec_memproj()

        @pl.when(sends_right(m))
        def _():
            mem_copy(m, to_slot(m)).start()

        @pl.when(has_left(m))
        def _():
            mem_copy(m, m).wait_recv()

        def sec_membuf():
            low = lax.broadcasted_iota(jnp.int32, (2 * NMEM, width), 0) < NMEM
            prev = mem_in[m].astype(F32)
            memk[0 : 2 * NMEM, :] = jnp.where(low, prev, memk[0 : 2 * NMEM, :])
            memv[0 : 2 * NMEM, :] = jnp.where(low, pltpu.roll(prev, NMEM, axis=0), memv[0 : 2 * NMEM, :])

        sec_membuf()

        def sec_attend():
            quad = 4
            qw = quad * (width // HEADS)
            win = LC + SEG
            lane = lax.broadcasted_iota(jnp.int32, (1, 128), 1)
            lane_seg = lane // SEG
            biases = []
            for i in range(segs):
                cnt = jnp.zeros((1, 128), jnp.int32)
                for j in range(left + 1):
                    cnt = jnp.where(lane_seg == j, near[segs - left + i + j], cnt)
                okay = (lane < win) & (lax.rem(lane, SEG) < cnt)
                for j in range(NMEM):
                    okay = okay | ((lane == win + i + j) & (near[i + j] > 0))
                biases.append(jnp.where(okay, 0.0, NEG))
            qlane = lax.broadcasted_iota(jnp.int32, (1, qw), 1) // (width // HEADS)
            sel = [jnp.where(qlane == h, 1.0, 0.0).astype(BF16) for h in range(quad)]

            def attend(g, c):
                col = pl.ds(pl.multiple_of(g * qw, qw), qw)
                mk = memk[:, col].astype(BF16)
                mv = memv[:, col].astype(BF16)
                for i in range(segs):
                    q = qbuf[i * SEG : (i + 1) * SEG, col]
                    q4 = jnp.concatenate([q * sel[h] for h in range(quad)], axis=0)
                    ks = jnp.concatenate([kbuf[i * SEG : i * SEG + win, col], mk], axis=0)
                    vs = jnp.concatenate([vbuf[i * SEG : i * SEG + win, col], mv], axis=0)
                    s = dot_nt(q4, ks) + biases[i]
                    e = jnp.exp(s - jnp.max(s, axis=-1, keepdims=True))
                    o = dot_nn(e.astype(BF16), vs) / jnp.sum(e, axis=-1, keepdims=True)
                    ctx = jnp.where(qlane == 0, o[0:SEG], 0.0)
                    for h in range(1, quad):
                        ctx = jnp.where(qlane == h, o[h * SEG : (h + 1) * SEG], ctx)
                    cbuf[i * SEG : (i + 1) * SEG, col] = ctx.astype(BF16)
                return c

            lax.fori_loop(0, width // qw, attend, 0, unroll=True)

        sec_attend()

        @pl.when(m == 0)
        def _():
            loads[3].wait()

        def sec_out():
            def project_out(n, c):
                col = pl.ds(pl.multiple_of(n * 256, 256), 256)
                r = xin[m, LC:total, col].astype(F32) + dot_nn(cbuf[...], wo[:, col])
                rbuf[:, col] = r.astype(BF16)
                return c

            lax.fori_loop(0, width // 256, project_out, 0, unroll=True)

        sec_out()

        def sec_rim():
            def row_mask(i):
                seg = i // 2
                cnt = count_of(m, seg)
                ids = lax.broadcasted_iota(jnp.int32, (16, 1), 0) + lax.rem(i, 2) * 16
                return jnp.where(ids < cnt, 1.0, 0.0)

            def conv_rows(i, c):
                r = pl.multiple_of(i * 16, 16)
                z = (layer_norm(rbuf[pl.ds(r, 16), :].astype(F32)) * row_mask(i)).astype(BF16)
                cext[pl.ds(r + SEG, 16), :] = z.astype(F32)
                return c

            lax.fori_loop(0, rows // 16, conv_rows, 0, unroll=True)
            rim_out[m] = cext[rows : rows + SEG, :].astype(BF16)

        sec_rim()

        @pl.when(sends_right(m))
        def _():
            rim_copy(m, to_slot(m)).start()

        sub = lax.broadcasted_iota(jnp.int32, (8, 128), 0)

        def conv_range(k0, k1):
            def body(cb, c):
                col = pl.ds(pl.multiple_of(cb * 128, 128), 128)
                a = {}

                def get(k):
                    if k not in a:
                        a[k] = cext[8 * k : 8 * k + 8, col]
                    return a[k]

                def tap(o):
                    return taps[o - 2, :, col]

                acc = {}
                for s in range(8):
                    offs = [o for o in range(s, KW + 2, 8) if 2 <= o <= KW + 1]
                    prev = None
                    for k in range(k0, k1 + (1 if s else 0)):
                        y = None
                        for o in offs:
                            term = tap(o) * get(k + o // 8)
                            y = term if y is None else y + term
                        if s == 0:
                            acc[k] = y
                            continue
                        y = pltpu.roll(y, 8 - s, axis=0)
                        if prev is not None:
                            acc[k - 1] = acc[k - 1] + jnp.where(sub < 8 - s, prev, y)
                        prev = y
                for k in range(k0, k1):
                    dbuf[8 * k : 8 * k + 8, col] = acc[k]
                return c

            lax.fori_loop(0, width // 128, body, 0)

        def gate_rows(lo, hi):
            for r in range(lo, hi, 16):
                z = layer_norm(dbuf[r : r + 16, :])
                gbuf[r : r + 16, :] = (z / (1.0 + jnp.exp(-z))).astype(BF16)

        vrow = lax.broadcasted_iota(jnp.int32, (rows, 1), 0)
        cnt_row = jnp.zeros((rows, 1), jnp.int32)
        for i in range(segs):
            cnt_row = jnp.where(vrow // SEG == i, near[segs + i], cnt_row)
        keep = jnp.where(lax.rem(vrow, SEG) < cnt_row, 1.0, 0.0)

        def point_rows(lo, hi):
            def project_point(n, c):
                col = pl.ds(pl.multiple_of(n * 256, 256), 256)
                y = rbuf[lo:hi, col].astype(F32) + dot_nn(gbuf[lo:hi, :], wp[:, col])
                obuf[m, lo:hi, col] = (y * keep[lo:hi]).astype(BF16)
                return c

            lax.fori_loop(0, width // 256, project_point, 0, unroll=True)

        def finish(n):
            lo, hi = PIECES[n]
            conv_range(lo // 8, hi // 8)
            gate_rows(lo, hi)
            point_rows(lo, hi)

        def send_piece(n):
            @pl.when(has_next)
            def _():
                piece_send(m, n).start()

        @pl.when(m == 0)
        def _():
            loads[5].wait()

        def sec_fin0():
            finish(0)

        sec_fin0()
        send_piece(0)

        @pl.when(has_next)
        def _():
            @pl.when(sends_right(m))
            def _():
                halo_send(m, to_slot(m)).start()


        @pl.when(has_left(m))
        def _():
            rim_copy(m, m).wait_recv()

        def sec_fin1():
            cext[0:SEG, :] = rim_in[m].astype(F32)
            finish(1)

        sec_fin1()
        send_piece(1)
        out_copy(m).start()
        return carry

    lax.fori_loop(0, micro, one_block, 0)

    for m in range(micro):
        out_copy(m).wait()

        @pl.when(has_next)
        def _():
            for n in range(len(PIECES)):
                piece_send(m, n).wait_send()

        @pl.when(sends_right(m))
        def _():
            mem_copy(m, to_slot(m)).wait_send()
            rim_copy(m, to_slot(m)).wait_send()

            @pl.when(has_next)
            def _():
                halo_send(m, to_slot(m)).wait_send()

            @pl.when(first_phase)
            def _():
                first_halo(m).wait_send()


def per_device(frames, frame_counts, w_query, w_key, w_value, w_out, conv_kernel, w_point):
    micro, rows, width = frames.shape
    shards = lax.axis_size("tm")
    phases = lax.axis_size("phase")
    dma = pltpu.SemaphoreType.DMA
    any_spec = pl.BlockSpec(memory_space=pltpu.HBM)
    mat = pltpu.VMEM((width, width), BF16)
    return pl.pallas_call(
        functools.partial(relay_kernel, shards, phases, micro, rows, width),
        out_shape=jax.ShapeDtypeStruct((1, micro, rows, width), BF16),
        in_specs=[pl.BlockSpec(memory_space=pltpu.SMEM)] + [any_spec] * 7,
        out_specs=any_spec,
        scratch_shapes=[
            mat, mat, mat, mat, pltpu.VMEM((KW, width), BF16), mat,
            pltpu.VMEM((micro, LC + rows, width), BF16),
            pltpu.VMEM((LC + rows + 16, width), BF16),
            pltpu.VMEM((LC + rows, width), BF16),
            pltpu.VMEM((LC + rows, width), BF16),
            pltpu.VMEM((rows + 16, width), BF16),
            pltpu.VMEM((rows, width), BF16),
            pltpu.VMEM((rows, width), BF16),
            pltpu.VMEM((SEG + rows, width), F32),
            pltpu.VMEM((rows, width), F32),
            pltpu.VMEM((rows, width), BF16),
            pltpu.VMEM((micro, rows, width), BF16),
            pltpu.VMEM((KW, 8, width), F32),
            pltpu.VMEM((micro, 2 * NMEM, width), BF16),
            pltpu.VMEM((micro, 2 * NMEM, width), BF16),
            pltpu.VMEM((SEG, width), F32),
            pltpu.VMEM((SEG, width), F32),
            pltpu.VMEM((micro, SEG, width), BF16),
            pltpu.VMEM((micro, SEG, width), BF16),
            dma((6,)), dma((micro,)), dma((micro,)),
            dma((micro, len(PIECES))), dma((micro, len(PIECES))), dma((2 * micro,)), dma((micro,)),
            dma((micro,)), dma((micro,)), dma((micro,)), dma((micro,)),
        ],
        compiler_params=pltpu.CompilerParams(
            collective_id=0, has_side_effects=True, vmem_limit_bytes=56 * 1024 * 1024
        ),
    )(frame_counts, frames, w_query, w_key, w_value, w_out, conv_kernel, w_point)


def solution(mesh):
    stage = P("phase", None, None)
    return jax.shard_map(
        per_device,
        mesh=mesh,
        in_specs=(P(None, "tm", None), P(), stage, stage, stage, stage, stage, stage),
        out_specs=P("phase", None, "tm", None),
        check_vma=False,
    )
```

```python
import functools

import jax
import jax.numpy as jnp
from jax import lax
from jax.experimental import pallas as pl
from jax.experimental.pallas import tpu as pltpu
from jax.sharding import PartitionSpec as P

HEADS = 16
SEG = 32
LC = 64
NMEM = 4
KW = 31
EPS = 1e-05
NEG = -1e30
PIECES = ((32, 128), (0, 32))
F32 = jnp.float32
BF16 = jnp.bfloat16
MESH = pl.DeviceIdType.MESH


def layer_norm(v):
    width = v.shape[-1]
    c = v - jnp.sum(v, axis=-1, keepdims=True) * (1.0 / width)
    s = jnp.sum(c * c, axis=-1, keepdims=True) * (1.0 / width)
    return c * lax.rsqrt(s + EPS)


def dot_nt(a, b):
    return lax.dot_general(a, b, (((1,), (1,)), ((), ())), preferred_element_type=F32)


def dot_nn(a, b):
    return jnp.dot(a, b, preferred_element_type=F32)


def relay_kernel(
    shards, phases, micro, rows, width,
    counts, frames, w_query, w_key, w_value, w_out, w_conv, w_point,
    out,
    wq, wk, wv, wo, wc, wp,
    xin, nbuf, kbuf, vbuf, qbuf, cbuf, rbuf, cext, dbuf, gbuf, obuf, taps,
    mem_out, mem_in, memk, memv, rim_out, rim_in,
    w_sem, fr_sem, out_sem,
    x_send, x_recv, xh_send, xh_recv, mem_send, mem_recv, rim_send, rim_recv,
):
    t = lax.axis_index("tm")
    p = lax.axis_index("phase")
    segs = rows // SEG
    span_segs = shards * segs
    t_next = lax.rem(t + 1, shards)
    t_prev = lax.rem(t + shards - 1, shards)
    p_next = lax.rem(p + 1, phases)
    p_prev = lax.rem(p + phases - 1, phases)
    first_phase = p == 0
    has_next = p < phases - 1
    last_shard = t == shards - 1
    wrap = jnp.where(last_shard, 1, 0)

    loads = [
        pltpu.make_async_copy(src.at[0], dst, w_sem.at[i])
        for i, (src, dst) in enumerate(
            [(w_key, wk), (w_value, wv), (w_query, wq), (w_out, wo), (w_conv, wc), (w_point, wp)]
        )
    ]

    def frame_load(m):
        return pltpu.make_async_copy(frames.at[m], xin.at[m, pl.ds(LC, rows)], fr_sem.at[m])

    @pl.when(first_phase)
    def _():
        for m in range(micro):
            frame_load(m).start()

    for load in loads:
        load.start()

    barrier = pltpu.get_barrier_semaphore()
    for dt, dp in (
        (t_next, p), (t_prev, p), (t, p_next), (t, p_prev), (t_next, p_next), (t_prev, p_prev)
    ):
        pl.semaphore_signal(barrier, inc=1, device_id=(dt, dp), device_id_type=MESH)
    pl.semaphore_wait(barrier, 6)

    def sends_right(m):
        return jnp.logical_or(t < shards - 1, m < micro - 1)

    def has_left(m):
        return jnp.logical_or(t > 0, m > 0)

    def first_halo(m):
        slot = jnp.minimum(m + wrap, micro - 1)
        return pltpu.make_async_remote_copy(
            src_ref=frames.at[m, pl.ds(rows - LC, LC)],
            dst_ref=xin.at[slot, pl.ds(0, LC)],
            send_sem=xh_send.at[micro + m], recv_sem=xh_recv.at[slot],
            device_id=(t_next, p), device_id_type=MESH,
        )

    def piece_send(m, n):
        lo, hi = PIECES[n]
        return pltpu.make_async_remote_copy(
            src_ref=obuf.at[m, pl.ds(lo, hi - lo)],
            dst_ref=xin.at[m, pl.ds(LC + lo, hi - lo)],
            send_sem=x_send.at[m, n], recv_sem=x_recv.at[m, n],
            device_id=(t, p_next), device_id_type=MESH,
        )

    def to_slot(m):
        return jnp.minimum(m + wrap, micro - 1)

    def halo_send(m, slot):
        return pltpu.make_async_remote_copy(
            src_ref=obuf.at[m, pl.ds(rows - LC, LC)],
            dst_ref=xin.at[slot, pl.ds(0, LC)],
            send_sem=xh_send.at[m], recv_sem=xh_recv.at[slot],
            device_id=(t_next, p_next), device_id_type=MESH,
        )

    def mem_copy(m, slot):
        return pltpu.make_async_remote_copy(
            src_ref=mem_out.at[m], dst_ref=mem_in.at[slot],
            send_sem=mem_send.at[m], recv_sem=mem_recv.at[slot],
            device_id=(t_next, p), device_id_type=MESH,
        )

    def rim_copy(m, slot):
        return pltpu.make_async_remote_copy(
            src_ref=rim_out.at[m], dst_ref=rim_in.at[slot],
            send_sem=rim_send.at[m], recv_sem=rim_recv.at[slot],
            device_id=(t_next, p), device_id_type=MESH,
        )

    def out_copy(m):
        return pltpu.make_async_copy(obuf.at[m], out.at[0, m], out_sem.at[m])

    @pl.when(first_phase)
    def _():
        for m in range(micro):
            @pl.when(sends_right(m))
            def _():
                first_halo(m).start()

    @pl.when(t == 0)
    def _():
        xin[0, 0:LC, :] = jnp.zeros((LC, width), BF16)
        mem_in[0] = jnp.zeros(mem_in.shape[1:], BF16)
        rim_in[0] = jnp.zeros(rim_in.shape[1:], BF16)

    memk[...] = jnp.zeros(memk.shape, F32)
    memv[...] = jnp.zeros(memv.shape, F32)

    def count_of(m, rel):
        s = m * span_segs + t * segs + rel
        safe = jnp.maximum(s, 0)
        value = counts[safe // span_segs, lax.rem(safe, span_segs)]
        return jnp.where(s >= 0, value, 0)

    def one_block(m, carry):
        near = [count_of(m, rel) for rel in range(-segs, segs)]
        left = LC // SEG

        total = LC + rows

        def norm_rows(lo, hi):
            for r in range(lo, hi, 16):
                nbuf[r : r + 16, :] = layer_norm(xin[m, r : r + 16, :].astype(F32)).astype(BF16)

        @pl.when(first_phase)
        def _():
            frame_load(m).wait()

        def wait_piece(n):
            @pl.when(jnp.logical_not(first_phase))
            def _():
                piece_send(m, n).wait_recv()

        wait_piece(0)

        def sec_norm2():
            norm_rows(LC + PIECES[0][0], LC + PIECES[0][1])

        sec_norm2()

        @pl.when(has_left(m))
        def _():
            halo_send(m, m).wait_recv()

        def sec_normh():
            norm_rows(0, LC)

        sec_normh()
        wait_piece(1)

        def sec_norm1():
            norm_rows(LC + PIECES[1][0], LC + PIECES[1][1])

        sec_norm1()

        @pl.when(m == 0)
        def _():
            for i in (0, 1, 2):
                loads[i].wait()

        def project(w, lhs, dst, finish):
            for n in range(width // 256):
                col = slice(n * 256, (n + 1) * 256)
                dst[:, col] = finish(dot_nn(lhs, w[:, col]))

        def plain(r):
            return r.astype(BF16)

        def scaled(r):
            return (r.astype(BF16).astype(F32) * 0.125).astype(BF16)

        nq = segs * HEADS
        hrow = lax.broadcasted_iota(jnp.int32, (HEADS, width), 0)
        hcol = lax.broadcasted_iota(jnp.int32, (HEADS, width), 1) // (width // HEADS)
        head_on = hrow == hcol

        def sec_memory():
            project(wk, nbuf[0:total, :], kbuf, plain)

            srow = lax.broadcasted_iota(jnp.int32, (16, rows), 0)
            scol = lax.broadcasted_iota(jnp.int32, (16, rows), 1)
            cnt_lane = jnp.zeros((16, rows), jnp.int32)
            cnt_col = jnp.ones((16, 1), jnp.int32)
            crow = lax.broadcasted_iota(jnp.int32, (16, 1), 0)
            for i in range(segs):
                cnt_lane = jnp.where(scol // SEG == i, near[segs + i], cnt_lane)
                cnt_col = jnp.where(crow == i, near[segs + i], cnt_col)
            pick = jnp.logical_and(srow == scol // SEG, lax.rem(scol, SEG) < cnt_lane)
            pick = jnp.where(pick, 1.0, 0.0).astype(BF16)
            summary = dot_nn(pick, nbuf[LC:total, :]) / cnt_col.astype(F32)
            nbuf[total : total + 16, :] = summary.astype(BF16)
            project(wq, nbuf[LC : total + 16, :], qbuf, scaled)

            sq = qbuf[rows : rows + 16, :].astype(F32)
            queries = jnp.concatenate(
                [
                    jnp.where(head_on, jnp.broadcast_to(sq[i : i + 1, :], (HEADS, width)), 0.0)
                    for i in range(segs)
                ],
                axis=0,
            ).astype(BF16)
            mrow = lax.broadcasted_iota(jnp.int32, (nq, total), 0) // HEADS
            mcol = lax.broadcasted_iota(jnp.int32, (nq, total), 1)
            mseg = mcol // SEG
            cnt_key = jnp.zeros((nq, total), jnp.int32)
            for i in range(left + segs):
                cnt_key = jnp.where(mseg == i, near[segs - left + i], cnt_key)
            ok = (mseg >= mrow) & (mseg <= mrow + left) & (lax.rem(mcol, SEG) < cnt_key)
            scores = jnp.where(ok, dot_nt(queries, kbuf[...]), NEG)
            project(wv, nbuf[0:total, :], vbuf, plain)
            expo = jnp.exp(scores - jnp.max(scores, axis=-1, keepdims=True))
            weights = (expo / jnp.sum(expo, axis=-1, keepdims=True)).astype(BF16)
            mixed = dot_nn(weights, vbuf[...])
            memory = jnp.concatenate(
                [
                    jnp.sum(jnp.where(head_on, mixed[i * HEADS : (i + 1) * HEADS, :], 0.0), axis=0, keepdims=True)
                    for i in range(segs)
                ]
                * 4,
                axis=0,
            ).astype(BF16)
            gbuf[0:16, :] = memory

        sec_memory()

        def sec_memproj():
            low = lax.broadcasted_iota(jnp.int32, (2 * NMEM, 256), 0) < NMEM

            def mem_project(n, c):
                col = pl.ds(pl.multiple_of(n * 256, 256), 256)
                mk = dot_nn(gbuf[0:16, :], wk[:, col])[0 : 2 * NMEM]
                mv = dot_nn(gbuf[0:16, :], wv[:, col])[0 : 2 * NMEM]
                mem_out[m, :, col] = jnp.where(low, mk, mv).astype(BF16)
                memk[0 : 2 * NMEM, col] = mk
                memv[0 : 2 * NMEM, col] = mv
                return c

            lax.fori_loop(0, width // 256, mem_project, 0, unroll=True)

        sec_memproj()

        @pl.when(sends_right(m))
        def _():
            mem_copy(m, to_slot(m)).start()

        @pl.when(m == 0)
        def _():
            loads[4].wait()
            for j in range(KW):
                taps[j] = jnp.broadcast_to(wc[j : j + 1, :].astype(F32), (8, width))

        @pl.when(has_left(m))
        def _():
            mem_copy(m, m).wait_recv()

        def sec_membuf():
            low = lax.broadcasted_iota(jnp.int32, (2 * NMEM, width), 0) < NMEM
            prev = mem_in[m].astype(F32)
            memk[0 : 2 * NMEM, :] = jnp.where(low, prev, memk[0 : 2 * NMEM, :])
            memv[0 : 2 * NMEM, :] = jnp.where(low, pltpu.roll(prev, NMEM, axis=0), memv[0 : 2 * NMEM, :])

        sec_membuf()

        def sec_attend():
            quad = 4
            qw = quad * (width // HEADS)
            win = LC + SEG
            lane = lax.broadcasted_iota(jnp.int32, (1, 128), 1)
            lane_seg = lane // SEG
            biases = []
            for i in range(segs):
                cnt = jnp.zeros((1, 128), jnp.int32)
                for j in range(left + 1):
                    cnt = jnp.where(lane_seg == j, near[segs - left + i + j], cnt)
                okay = (lane < win) & (lax.rem(lane, SEG) < cnt)
                for j in range(NMEM):
                    okay = okay | ((lane == win + i + j) & (near[i + j] > 0))
                biases.append(jnp.where(okay, 0.0, NEG))
            qlane = lax.broadcasted_iota(jnp.int32, (1, qw), 1) // (width // HEADS)
            sel = [jnp.where(qlane == h, 1.0, 0.0).astype(BF16) for h in range(quad)]

            def attend(g, c):
                col = pl.ds(pl.multiple_of(g * qw, qw), qw)
                mk = memk[:, col].astype(BF16)
                mv = memv[:, col].astype(BF16)
                for i in range(segs):
                    q = qbuf[i * SEG : (i + 1) * SEG, col]
                    q4 = jnp.concatenate([q * sel[h] for h in range(quad)], axis=0)
                    ks = jnp.concatenate([kbuf[i * SEG : i * SEG + win, col], mk], axis=0)
                    vs = jnp.concatenate([vbuf[i * SEG : i * SEG + win, col], mv], axis=0)
                    s = dot_nt(q4, ks) + biases[i]
                    e = jnp.exp(s - jnp.max(s, axis=-1, keepdims=True))
                    o = dot_nn(e.astype(BF16), vs) / jnp.sum(e, axis=-1, keepdims=True)
                    ctx = jnp.where(qlane == 0, o[0:SEG], 0.0)
                    for h in range(1, quad):
                        ctx = jnp.where(qlane == h, o[h * SEG : (h + 1) * SEG], ctx)
                    cbuf[i * SEG : (i + 1) * SEG, col] = ctx.astype(BF16)
                return c

            lax.fori_loop(0, width // qw, attend, 0, unroll=True)

        sec_attend()

        @pl.when(m == 0)
        def _():
            loads[3].wait()

        def sec_out():
            def project_out(n, c):
                col = pl.ds(pl.multiple_of(n * 256, 256), 256)
                r = xin[m, LC:total, col].astype(F32) + dot_nn(cbuf[...], wo[:, col])
                rbuf[:, col] = r.astype(BF16)
                return c

            lax.fori_loop(0, width // 256, project_out, 0, unroll=True)

        sec_out()

        def sec_rim():
            def row_mask(i):
                seg = i // 2
                cnt = count_of(m, seg)
                ids = lax.broadcasted_iota(jnp.int32, (16, 1), 0) + lax.rem(i, 2) * 16
                return jnp.where(ids < cnt, 1.0, 0.0)

            def conv_rows(i, c):
                r = pl.multiple_of(i * 16, 16)
                z = (layer_norm(rbuf[pl.ds(r, 16), :].astype(F32)) * row_mask(i)).astype(BF16)
                cext[pl.ds(r + SEG, 16), :] = z.astype(F32)
                return c

            lax.fori_loop(0, rows // 16, conv_rows, 0, unroll=True)
            rim_out[m] = cext[rows : rows + SEG, :].astype(BF16)

        sec_rim()

        @pl.when(sends_right(m))
        def _():
            rim_copy(m, to_slot(m)).start()

        sub = lax.broadcasted_iota(jnp.int32, (8, 128), 0)

        def conv_range(k0, k1, a0, a1, more, unroll):
            def body(cb, c):
                col = pl.ds(pl.multiple_of(cb * 128, 128), 128)
                a = {}

                def get(k):
                    if k not in a:
                        a[k] = cext[8 * k : 8 * k + 8, col]
                    return a[k]

                acc = {k: dbuf[8 * k : 8 * k + 8, col] if more else None for k in range(k0, k1)}

                def add(k, term):
                    acc[k] = term if acc[k] is None else acc[k] + term

                for s in range(8):
                    offs = [o for o in range(s, KW + 2, 8) if 2 <= o <= KW + 1]
                    prev = None
                    for k in range(k0, k1 + (1 if s else 0)):
                        y = None
                        for o in offs:
                            if a0 <= k + o // 8 < a1:
                                term = taps[o - 2, :, col] * get(k + o // 8)
                                y = term if y is None else y + term
                        if s == 0:
                            if y is not None:
                                add(k, y)
                            continue
                        if y is not None:
                            y = pltpu.roll(y, 8 - s, axis=0)
                        if k > k0 and not (prev is None and y is None):
                            head = 0.0 if prev is None else prev
                            tail = 0.0 if y is None else y
                            add(k - 1, jnp.where(sub < 8 - s, head, tail))
                        prev = y
                for k in range(k0, k1):
                    if acc[k] is not None:
                        dbuf[8 * k : 8 * k + 8, col] = acc[k]
                return c

            lax.fori_loop(0, width // 128, body, 0, unroll=unroll)

        first = SEG // 8
        every = (SEG + rows) // 8

        def gate_rows(lo, hi):
            for r in range(lo, hi, 16):
                z = layer_norm(dbuf[r : r + 16, :])
                gbuf[r : r + 16, :] = (z / (1.0 + jnp.exp(-z))).astype(BF16)

        vrow = lax.broadcasted_iota(jnp.int32, (rows, 1), 0)
        cnt_row = jnp.zeros((rows, 1), jnp.int32)
        for i in range(segs):
            cnt_row = jnp.where(vrow // SEG == i, near[segs + i], cnt_row)
        keep = jnp.where(lax.rem(vrow, SEG) < cnt_row, 1.0, 0.0)

        def point_rows(lo, hi):
            def project_point(n, c):
                col = pl.ds(pl.multiple_of(n * 256, 256), 256)
                y = rbuf[lo:hi, col].astype(F32) + dot_nn(gbuf[lo:hi, :], wp[:, col])
                obuf[m, lo:hi, col] = (y * keep[lo:hi]).astype(BF16)
                return c

            lax.fori_loop(0, width // 256, project_point, 0, unroll=True)

        def finish(n):
            lo, hi = PIECES[n]
            gate_rows(lo, hi)
            point_rows(lo, hi)

        def send_piece(n):
            @pl.when(has_next)
            def _():
                piece_send(m, n).start()

        @pl.when(m == 0)
        def _():
            loads[5].wait()

        def sec_fin0():
            conv_range(first, rows // 8, first, every, False, 4)
            finish(0)

        sec_fin0()
        send_piece(0)

        @pl.when(has_next)
        def _():
            @pl.when(sends_right(m))
            def _():
                halo_send(m, to_slot(m)).start()


        def sec_pre():
            conv_range(0, first, first, every, False, 4)

        sec_pre()

        @pl.when(has_left(m))
        def _():
            rim_copy(m, m).wait_recv()

        def sec_fin1():
            cext[0:SEG, :] = rim_in[m].astype(F32)
            conv_range(0, first, 0, first, True, 4)
            finish(1)

        sec_fin1()
        send_piece(1)
        out_copy(m).start()
        return carry

    lax.fori_loop(0, micro, one_block, 0)

    for m in range(micro):
        out_copy(m).wait()

        @pl.when(has_next)
        def _():
            for n in range(len(PIECES)):
                piece_send(m, n).wait_send()

        @pl.when(sends_right(m))
        def _():
            mem_copy(m, to_slot(m)).wait_send()
            rim_copy(m, to_slot(m)).wait_send()

            @pl.when(has_next)
            def _():
                halo_send(m, to_slot(m)).wait_send()

            @pl.when(first_phase)
            def _():
                first_halo(m).wait_send()


def per_device(frames, frame_counts, w_query, w_key, w_value, w_out, conv_kernel, w_point):
    micro, rows, width = frames.shape
    shards = lax.axis_size("tm")
    phases = lax.axis_size("phase")
    dma = pltpu.SemaphoreType.DMA
    any_spec = pl.BlockSpec(memory_space=pltpu.HBM)
    mat = pltpu.VMEM((width, width), BF16)
    return pl.pallas_call(
        functools.partial(relay_kernel, shards, phases, micro, rows, width),
        out_shape=jax.ShapeDtypeStruct((1, micro, rows, width), BF16),
        in_specs=[pl.BlockSpec(memory_space=pltpu.SMEM)] + [any_spec] * 7,
        out_specs=any_spec,
        scratch_shapes=[
            mat, mat, mat, mat, pltpu.VMEM((KW, width), BF16), mat,
            pltpu.VMEM((micro, LC + rows, width), BF16),
            pltpu.VMEM((LC + rows + 16, width), BF16),
            pltpu.VMEM((LC + rows, width), BF16),
            pltpu.VMEM((LC + rows, width), BF16),
            pltpu.VMEM((rows + 16, width), BF16),
            pltpu.VMEM((rows, width), BF16),
            pltpu.VMEM((rows, width), BF16),
            pltpu.VMEM((SEG + rows, width), F32),
            pltpu.VMEM((rows, width), F32),
            pltpu.VMEM((rows, width), BF16),
            pltpu.VMEM((micro, rows, width), BF16),
            pltpu.VMEM((KW, 8, width), F32),
            pltpu.VMEM((micro, 2 * NMEM, width), BF16),
            pltpu.VMEM((micro, 2 * NMEM, width), BF16),
            pltpu.VMEM((SEG, width), F32),
            pltpu.VMEM((SEG, width), F32),
            pltpu.VMEM((micro, SEG, width), BF16),
            pltpu.VMEM((micro, SEG, width), BF16),
            dma((6,)), dma((micro,)), dma((micro,)),
            dma((micro, len(PIECES))), dma((micro, len(PIECES))), dma((2 * micro,)), dma((micro,)),
            dma((micro,)), dma((micro,)), dma((micro,)), dma((micro,)),
        ],
        compiler_params=pltpu.CompilerParams(
            collective_id=0, has_side_effects=True, vmem_limit_bytes=56 * 1024 * 1024
        ),
    )(frame_counts, frames, w_query, w_key, w_value, w_out, conv_kernel, w_point)


def solution(mesh):
    stage = P("phase", None, None)
    return jax.shard_map(
        per_device,
        mesh=mesh,
        in_specs=(P(None, "tm", None), P(), stage, stage, stage, stage, stage, stage),
        out_specs=P("phase", None, "tm", None),
        check_vma=False,
    )
```

```python
import functools

import jax
import jax.numpy as jnp
from jax import lax
from jax.experimental import pallas as pl
from jax.experimental.pallas import tpu as pltpu
from jax.sharding import PartitionSpec as P

HEADS = 16
SEG = 32
LC = 64
NMEM = 4
KW = 31
EPS = 1e-05
NEG = -1e30
PIECES = ((64, 128), (0, 64))
F32 = jnp.float32
BF16 = jnp.bfloat16
MESH = pl.DeviceIdType.MESH


def layer_norm(v):
    width = v.shape[-1]
    c = v - jnp.sum(v, axis=-1, keepdims=True) * (1.0 / width)
    s = jnp.sum(c * c, axis=-1, keepdims=True) * (1.0 / width)
    return c * lax.rsqrt(s + EPS)


def dot_nt(a, b):
    return lax.dot_general(a, b, (((1,), (1,)), ((), ())), preferred_element_type=F32)


def dot_nn(a, b):
    return jnp.dot(a, b, preferred_element_type=F32)


def relay_kernel(
    shards, phases, micro, rows, width,
    counts, frames, w_query, w_key, w_value, w_out, w_conv, w_point,
    out,
    wq, wk, wv, wo, wc, wp,
    xin, nbuf, kbuf, vbuf, qbuf, cbuf, rbuf, cext, dbuf, gbuf, obuf, taps,
    mem_out, mem_in, memk, memv, rim_out, rim_in,
    w_sem, fr_sem, out_sem,
    x_send, x_recv, xh_send, xh_recv, mem_send, mem_recv, rim_send, rim_recv,
):
    t = lax.axis_index("tm")
    p = lax.axis_index("phase")
    segs = rows // SEG
    span_segs = shards * segs
    t_next = lax.rem(t + 1, shards)
    t_prev = lax.rem(t + shards - 1, shards)
    p_next = lax.rem(p + 1, phases)
    p_prev = lax.rem(p + phases - 1, phases)
    first_phase = p == 0
    has_next = p < phases - 1
    last_shard = t == shards - 1
    wrap = jnp.where(last_shard, 1, 0)

    loads = [
        pltpu.make_async_copy(src.at[0], dst, w_sem.at[i])
        for i, (src, dst) in enumerate(
            [(w_key, wk), (w_value, wv), (w_query, wq), (w_out, wo), (w_conv, wc), (w_point, wp)]
        )
    ]

    def frame_load(m):
        return pltpu.make_async_copy(frames.at[m], xin.at[m, pl.ds(LC, rows)], fr_sem.at[m])

    @pl.when(first_phase)
    def _():
        for m in range(micro):
            frame_load(m).start()

    for load in loads:
        load.start()

    barrier = pltpu.get_barrier_semaphore()
    for dt, dp in (
        (t_next, p), (t_prev, p), (t, p_next), (t, p_prev), (t_next, p_next), (t_prev, p_prev)
    ):
        pl.semaphore_signal(barrier, inc=1, device_id=(dt, dp), device_id_type=MESH)
    pl.semaphore_wait(barrier, 6)

    def sends_right(m):
        return jnp.logical_or(t < shards - 1, m < micro - 1)

    def has_left(m):
        return jnp.logical_or(t > 0, m > 0)

    def first_halo(m):
        slot = jnp.minimum(m + wrap, micro - 1)
        return pltpu.make_async_remote_copy(
            src_ref=frames.at[m, pl.ds(rows - LC, LC)],
            dst_ref=xin.at[slot, pl.ds(0, LC)],
            send_sem=xh_send.at[micro + m], recv_sem=xh_recv.at[slot],
            device_id=(t_next, p), device_id_type=MESH,
        )

    def piece_send(m, n):
        lo, hi = PIECES[n]
        return pltpu.make_async_remote_copy(
            src_ref=obuf.at[m, pl.ds(lo, hi - lo)],
            dst_ref=xin.at[m, pl.ds(LC + lo, hi - lo)],
            send_sem=x_send.at[m, n], recv_sem=x_recv.at[m, n],
            device_id=(t, p_next), device_id_type=MESH,
        )

    def to_slot(m):
        return jnp.minimum(m + wrap, micro - 1)

    def halo_send(m, slot):
        return pltpu.make_async_remote_copy(
            src_ref=obuf.at[m, pl.ds(rows - LC, LC)],
            dst_ref=xin.at[slot, pl.ds(0, LC)],
            send_sem=xh_send.at[m], recv_sem=xh_recv.at[slot],
            device_id=(t_next, p_next), device_id_type=MESH,
        )

    def mem_copy(m, slot):
        return pltpu.make_async_remote_copy(
            src_ref=mem_out.at[m], dst_ref=mem_in.at[slot],
            send_sem=mem_send.at[m], recv_sem=mem_recv.at[slot],
            device_id=(t_next, p), device_id_type=MESH,
        )

    def rim_copy(m, slot):
        return pltpu.make_async_remote_copy(
            src_ref=rim_out.at[m], dst_ref=rim_in.at[slot],
            send_sem=rim_send.at[m], recv_sem=rim_recv.at[slot],
            device_id=(t_next, p), device_id_type=MESH,
        )

    def out_copy(m):
        return pltpu.make_async_copy(obuf.at[m], out.at[0, m], out_sem.at[m])

    @pl.when(first_phase)
    def _():
        for m in range(micro):
            @pl.when(sends_right(m))
            def _():
                first_halo(m).start()

    @pl.when(t == 0)
    def _():
        xin[0, 0:LC, :] = jnp.zeros((LC, width), BF16)
        mem_in[0] = jnp.zeros(mem_in.shape[1:], BF16)
        rim_in[0] = jnp.zeros(rim_in.shape[1:], BF16)

    memk[...] = jnp.zeros(memk.shape, F32)
    memv[...] = jnp.zeros(memv.shape, F32)

    def count_of(m, rel):
        s = m * span_segs + t * segs + rel
        safe = jnp.maximum(s, 0)
        value = counts[safe // span_segs, lax.rem(safe, span_segs)]
        return jnp.where(s >= 0, value, 0)

    def one_block(m, carry):
        near = [count_of(m, rel) for rel in range(-segs, segs)]
        left = LC // SEG

        total = LC + rows

        def norm_rows(lo, hi):
            for r in range(lo, hi, 16):
                nbuf[r : r + 16, :] = layer_norm(xin[m, r : r + 16, :].astype(F32)).astype(BF16)

        @pl.when(first_phase)
        def _():
            frame_load(m).wait()

        def wait_piece(n):
            @pl.when(jnp.logical_not(first_phase))
            def _():
                piece_send(m, n).wait_recv()

        wait_piece(0)

        def sec_norm2():
            norm_rows(LC + PIECES[0][0], LC + PIECES[0][1])

        sec_norm2()

        @pl.when(has_left(m))
        def _():
            halo_send(m, m).wait_recv()

        wait_piece(1)

        def sec_norm1():
            norm_rows(0, LC)
            norm_rows(LC + PIECES[1][0], LC + PIECES[1][1])

        sec_norm1()

        @pl.when(m == 0)
        def _():
            for i in (0, 1, 2):
                loads[i].wait()

        def project(w, lhs, dst, finish):
            for n in range(width // 256):
                col = slice(n * 256, (n + 1) * 256)
                dst[:, col] = finish(dot_nn(lhs, w[:, col]))

        def plain(r):
            return r.astype(BF16)

        def scaled(r):
            return (r.astype(BF16).astype(F32) * 0.125).astype(BF16)

        nq = segs * HEADS
        hrow = lax.broadcasted_iota(jnp.int32, (HEADS, width), 0)
        hcol = lax.broadcasted_iota(jnp.int32, (HEADS, width), 1) // (width // HEADS)
        head_on = hrow == hcol

        def sec_memory():
            project(wk, nbuf[0:total, :], kbuf, plain)

            srow = lax.broadcasted_iota(jnp.int32, (16, rows), 0)
            scol = lax.broadcasted_iota(jnp.int32, (16, rows), 1)
            cnt_lane = jnp.zeros((16, rows), jnp.int32)
            cnt_col = jnp.ones((16, 1), jnp.int32)
            crow = lax.broadcasted_iota(jnp.int32, (16, 1), 0)
            for i in range(segs):
                cnt_lane = jnp.where(scol // SEG == i, near[segs + i], cnt_lane)
                cnt_col = jnp.where(crow == i, near[segs + i], cnt_col)
            pick = jnp.logical_and(srow == scol // SEG, lax.rem(scol, SEG) < cnt_lane)
            pick = jnp.where(pick, 1.0, 0.0).astype(BF16)
            summary = dot_nn(pick, nbuf[LC:total, :]) / cnt_col.astype(F32)
            nbuf[total : total + 16, :] = summary.astype(BF16)
            project(wq, nbuf[LC : total + 16, :], qbuf, scaled)

            sq = qbuf[rows : rows + 16, :].astype(F32)
            queries = jnp.concatenate(
                [
                    jnp.where(head_on, jnp.broadcast_to(sq[i : i + 1, :], (HEADS, width)), 0.0)
                    for i in range(segs)
                ],
                axis=0,
            ).astype(BF16)
            mrow = lax.broadcasted_iota(jnp.int32, (nq, total), 0) // HEADS
            mcol = lax.broadcasted_iota(jnp.int32, (nq, total), 1)
            mseg = mcol // SEG
            cnt_key = jnp.zeros((nq, total), jnp.int32)
            for i in range(left + segs):
                cnt_key = jnp.where(mseg == i, near[segs - left + i], cnt_key)
            ok = (mseg >= mrow) & (mseg <= mrow + left) & (lax.rem(mcol, SEG) < cnt_key)
            scores = jnp.where(ok, dot_nt(queries, kbuf[...]), NEG)
            project(wv, nbuf[0:total, :], vbuf, plain)
            expo = jnp.exp(scores - jnp.max(scores, axis=-1, keepdims=True))
            weights = (expo / jnp.sum(expo, axis=-1, keepdims=True)).astype(BF16)
            mixed = dot_nn(weights, vbuf[...])
            memory = jnp.concatenate(
                [
                    jnp.sum(jnp.where(head_on, mixed[i * HEADS : (i + 1) * HEADS, :], 0.0), axis=0, keepdims=True)
                    for i in range(segs)
                ]
                * 4,
                axis=0,
            ).astype(BF16)
            gbuf[0:16, :] = memory

        sec_memory()

        def sec_memproj():
            low = lax.broadcasted_iota(jnp.int32, (2 * NMEM, 256), 0) < NMEM

            def mem_project(n, c):
                col = pl.ds(pl.multiple_of(n * 256, 256), 256)
                mk = dot_nn(gbuf[0:16, :], wk[:, col])[0 : 2 * NMEM]
                mv = dot_nn(gbuf[0:16, :], wv[:, col])[0 : 2 * NMEM]
                mem_out[m, :, col] = jnp.where(low, mk, mv).astype(BF16)
                memk[0 : 2 * NMEM, col] = mk
                memv[0 : 2 * NMEM, col] = mv
                return c

            lax.fori_loop(0, width // 256, mem_project, 0, unroll=True)

        sec_memproj()

        @pl.when(sends_right(m))
        def _():
            mem_copy(m, to_slot(m)).start()

        @pl.when(m == 0)
        def _():
            for i in (3, 4, 5):
                loads[i].wait()
            for j in range(KW):
                taps[j] = jnp.broadcast_to(wc[j : j + 1, :].astype(F32), (8, width))

        quad = 4
        qw = quad * (width // HEADS)
        win = LC + SEG
        lane = lax.broadcasted_iota(jnp.int32, (1, 128), 1)
        lane_seg = lane // SEG
        biases = []
        for i in range(segs):
            cnt = jnp.zeros((1, 128), jnp.int32)
            for j in range(left + 1):
                cnt = jnp.where(lane_seg == j, near[segs - left + i + j], cnt)
            okay = (lane < win) & (lax.rem(lane, SEG) < cnt)
            for j in range(NMEM):
                okay = okay | ((lane == win + i + j) & (near[i + j] > 0))
            biases.append(jnp.where(okay, 0.0, NEG))
        qlane = lax.broadcasted_iota(jnp.int32, (1, qw), 1) // (width // HEADS)
        sel = [jnp.where(qlane == h, 1.0, 0.0).astype(BF16) for h in range(quad)]

        def attend(g):
            col = slice(g * qw, (g + 1) * qw)
            mk = memk[:, col].astype(BF16)
            mv = memv[:, col].astype(BF16)
            for i in range(segs):
                q = qbuf[i * SEG : (i + 1) * SEG, col]
                q4 = jnp.concatenate([q * sel[h] for h in range(quad)], axis=0)
                ks = jnp.concatenate([kbuf[i * SEG : i * SEG + win, col], mk], axis=0)
                vs = jnp.concatenate([vbuf[i * SEG : i * SEG + win, col], mv], axis=0)
                s = dot_nt(q4, ks) + biases[i]
                e = jnp.exp(s - jnp.max(s, axis=-1, keepdims=True))
                o = dot_nn(e.astype(BF16), vs) / jnp.sum(e, axis=-1, keepdims=True)
                ctx = jnp.where(qlane == 0, o[0:SEG], 0.0)
                for h in range(1, quad):
                    ctx = jnp.where(qlane == h, o[h * SEG : (h + 1) * SEG], ctx)
                cbuf[i * SEG : (i + 1) * SEG, col] = ctx.astype(BF16)

        def project_out(lo, hi):
            for n in range(width // 256):
                col = slice(n * 256, (n + 1) * 256)
                r = xin[m, LC + lo : LC + hi, col].astype(F32) + dot_nn(cbuf[lo:hi, :], wo[:, col])
                rbuf[lo:hi, col] = r.astype(BF16)

        vrow = lax.broadcasted_iota(jnp.int32, (rows, 1), 0)
        cnt_row = jnp.zeros((rows, 1), jnp.int32)
        for i in range(segs):
            cnt_row = jnp.where(vrow // SEG == i, near[segs + i], cnt_row)
        keep = jnp.where(lax.rem(vrow, SEG) < cnt_row, 1.0, 0.0)

        def conv_input(lo, hi):
            for r in range(lo, hi, 16):
                z = (layer_norm(rbuf[r : r + 16, :].astype(F32)) * keep[r : r + 16]).astype(BF16)
                cext[r + SEG : r + SEG + 16, :] = z.astype(F32)
                if r >= rows - SEG:
                    rim_out[m, r - rows + SEG : r - rows + SEG + 16, :] = z

        @pl.when(has_left(m))
        def _():
            mem_copy(m, m).wait_recv()

        def sec_membuf():
            low = lax.broadcasted_iota(jnp.int32, (2 * NMEM, width), 0) < NMEM
            prev = mem_in[m].astype(F32)
            memk[0 : 2 * NMEM, :] = jnp.where(low, prev, memk[0 : 2 * NMEM, :])
            memv[0 : 2 * NMEM, :] = jnp.where(low, pltpu.roll(prev, NMEM, axis=0), memv[0 : 2 * NMEM, :])

        sec_membuf()

        def sec_attend():
            for g in range(width // qw):
                attend(g)
            project_out(0, rows)
            conv_input(0, rows)

        sec_attend()

        @pl.when(sends_right(m))
        def _():
            rim_copy(m, to_slot(m)).start()

        sub = lax.broadcasted_iota(jnp.int32, (8, 128), 0)

        def conv_range(k0, k1, a0, a1, more, unroll):
            def body(cb, c):
                col = pl.ds(pl.multiple_of(cb * 128, 128), 128)
                a = {}

                def get(k):
                    if k not in a:
                        a[k] = cext[8 * k : 8 * k + 8, col]
                    return a[k]

                acc = {k: dbuf[8 * k : 8 * k + 8, col] if more else None for k in range(k0, k1)}

                def add(k, term):
                    acc[k] = term if acc[k] is None else acc[k] + term

                for s in range(8):
                    offs = [o for o in range(s, KW + 2, 8) if 2 <= o <= KW + 1]
                    prev = None
                    for k in range(k0, k1 + (1 if s else 0)):
                        y = None
                        for o in offs:
                            if a0 <= k + o // 8 < a1:
                                term = taps[o - 2, :, col] * get(k + o // 8)
                                y = term if y is None else y + term
                        if s == 0:
                            if y is not None:
                                add(k, y)
                            continue
                        if y is not None:
                            y = pltpu.roll(y, 8 - s, axis=0)
                        if k > k0 and not (prev is None and y is None):
                            head = 0.0 if prev is None else prev
                            tail = 0.0 if y is None else y
                            add(k - 1, jnp.where(sub < 8 - s, head, tail))
                        prev = y
                for k in range(k0, k1):
                    if acc[k] is not None:
                        dbuf[8 * k : 8 * k + 8, col] = acc[k]
                return c

            lax.fori_loop(0, width // 128, body, 0, unroll=unroll)

        first = SEG // 8
        every = (SEG + rows) // 8

        def gate_rows(lo, hi):
            for r in range(lo, hi, 16):
                z = layer_norm(dbuf[r : r + 16, :])
                gbuf[r : r + 16, :] = (z / (1.0 + jnp.exp(-z))).astype(BF16)

        def point_rows(lo, hi):
            def project_point(n, c):
                col = pl.ds(pl.multiple_of(n * 256, 256), 256)
                y = rbuf[lo:hi, col].astype(F32) + dot_nn(gbuf[lo:hi, :], wp[:, col])
                obuf[m, lo:hi, col] = (y * keep[lo:hi]).astype(BF16)
                return c

            lax.fori_loop(0, width // 256, project_point, 0, unroll=True)

        def finish(n):
            lo, hi = PIECES[n]
            gate_rows(lo, hi)
            point_rows(lo, hi)

        def send_piece(n):
            @pl.when(has_next)
            def _():
                piece_send(m, n).start()

        def sec_fin0():
            conv_range(PIECES[0][0] // 8, rows // 8, first, every, False, 4)
            finish(0)

        sec_fin0()
        send_piece(0)

        @pl.when(has_next)
        def _():
            @pl.when(sends_right(m))
            def _():
                halo_send(m, to_slot(m)).start()


        def sec_pre():
            conv_range(first, PIECES[0][0] // 8, first, every, False, 4)
            conv_range(0, first, first, every, False, 4)

        sec_pre()

        @pl.when(has_left(m))
        def _():
            rim_copy(m, m).wait_recv()

        def sec_fin1():
            cext[0:SEG, :] = rim_in[m].astype(F32)
            conv_range(0, first, 0, first, True, 4)
            finish(1)

        sec_fin1()
        send_piece(1)
        out_copy(m).start()
        return carry

    lax.fori_loop(0, micro, one_block, 0)

    for m in range(micro):
        out_copy(m).wait()

        @pl.when(has_next)
        def _():
            for n in range(len(PIECES)):
                piece_send(m, n).wait_send()

        @pl.when(sends_right(m))
        def _():
            mem_copy(m, to_slot(m)).wait_send()
            rim_copy(m, to_slot(m)).wait_send()

            @pl.when(has_next)
            def _():
                halo_send(m, to_slot(m)).wait_send()

            @pl.when(first_phase)
            def _():
                first_halo(m).wait_send()


def per_device(frames, frame_counts, w_query, w_key, w_value, w_out, conv_kernel, w_point):
    micro, rows, width = frames.shape
    shards = lax.axis_size("tm")
    phases = lax.axis_size("phase")
    dma = pltpu.SemaphoreType.DMA
    any_spec = pl.BlockSpec(memory_space=pltpu.HBM)
    mat = pltpu.VMEM((width, width), BF16)
    return pl.pallas_call(
        functools.partial(relay_kernel, shards, phases, micro, rows, width),
        out_shape=jax.ShapeDtypeStruct((1, micro, rows, width), BF16),
        in_specs=[pl.BlockSpec(memory_space=pltpu.SMEM)] + [any_spec] * 7,
        out_specs=any_spec,
        scratch_shapes=[
            mat, mat, mat, mat, pltpu.VMEM((KW, width), BF16), mat,
            pltpu.VMEM((micro, LC + rows, width), BF16),
            pltpu.VMEM((LC + rows + 16, width), BF16),
            pltpu.VMEM((LC + rows, width), BF16),
            pltpu.VMEM((LC + rows, width), BF16),
            pltpu.VMEM((rows + 16, width), BF16),
            pltpu.VMEM((rows, width), BF16),
            pltpu.VMEM((rows, width), BF16),
            pltpu.VMEM((SEG + rows, width), F32),
            pltpu.VMEM((rows, width), F32),
            pltpu.VMEM((rows, width), BF16),
            pltpu.VMEM((micro, rows, width), BF16),
            pltpu.VMEM((KW, 8, width), F32),
            pltpu.VMEM((micro, 2 * NMEM, width), BF16),
            pltpu.VMEM((micro, 2 * NMEM, width), BF16),
            pltpu.VMEM((SEG, width), F32),
            pltpu.VMEM((SEG, width), F32),
            pltpu.VMEM((micro, SEG, width), BF16),
            pltpu.VMEM((micro, SEG, width), BF16),
            dma((6,)), dma((micro,)), dma((micro,)),
            dma((micro, len(PIECES))), dma((micro, len(PIECES))), dma((2 * micro,)), dma((micro,)),
            dma((micro,)), dma((micro,)), dma((micro,)), dma((micro,)),
        ],
        compiler_params=pltpu.CompilerParams(
            collective_id=0, has_side_effects=True, vmem_limit_bytes=56 * 1024 * 1024
        ),
    )(frame_counts, frames, w_query, w_key, w_value, w_out, conv_kernel, w_point)


def solution(mesh):
    stage = P("phase", None, None)
    return jax.shard_map(
        per_device,
        mesh=mesh,
        in_specs=(P(None, "tm", None), P(), stage, stage, stage, stage, stage, stage),
        out_specs=P("phase", None, "tm", None),
        check_vma=False,
    )
```

```python
import functools

import jax
import jax.numpy as jnp
from jax import lax
from jax.experimental import pallas as pl
from jax.experimental.pallas import tpu as pltpu
from jax.sharding import PartitionSpec as P

HEADS = 16
SEG = 32
LC = 64
NMEM = 4
KW = 31
EPS = 1e-05
NEG = -1e30
PIECES = ((64, 128), (0, 64))
F32 = jnp.float32
BF16 = jnp.bfloat16
MESH = pl.DeviceIdType.MESH


def layer_norm(v):
    width = v.shape[-1]
    c = v - jnp.sum(v, axis=-1, keepdims=True) * (1.0 / width)
    s = jnp.sum(c * c, axis=-1, keepdims=True) * (1.0 / width)
    return c * lax.rsqrt(s + EPS)


def dot_nt(a, b):
    return lax.dot_general(a, b, (((1,), (1,)), ((), ())), preferred_element_type=F32)


def dot_nn(a, b):
    return jnp.dot(a, b, preferred_element_type=F32)


def relay_kernel(
    shards, phases, micro, rows, width,
    counts, frames, w_query, w_key, w_value, w_out, w_conv, w_point,
    out,
    wq, wk, wv, wo, wc, wp,
    xin, nbuf, kbuf, vbuf, qbuf, cbuf, rbuf, cext, dbuf, gbuf, obuf, taps,
    mem_out, mem_in, memk, memv, rim_out, rim_in,
    w_sem, fr_sem, out_sem,
    x_send, x_recv, xh_send, xh_recv, mem_send, mem_recv, rim_send, rim_recv,
):
    t = lax.axis_index("tm")
    p = lax.axis_index("phase")
    segs = rows // SEG
    span_segs = shards * segs
    t_next = lax.rem(t + 1, shards)
    t_prev = lax.rem(t + shards - 1, shards)
    p_next = lax.rem(p + 1, phases)
    p_prev = lax.rem(p + phases - 1, phases)
    first_phase = p == 0
    has_next = p < phases - 1
    last_shard = t == shards - 1
    wrap = jnp.where(last_shard, 1, 0)

    barrier = pltpu.get_barrier_semaphore()
    for dt, dp in (
        (t_next, p), (t_prev, p), (t, p_next), (t, p_prev), (t_next, p_next), (t_prev, p_prev)
    ):
        pl.semaphore_signal(barrier, inc=1, device_id=(dt, dp), device_id_type=MESH)

    loads = [
        pltpu.make_async_copy(src.at[0], dst, w_sem.at[i])
        for i, (src, dst) in enumerate(
            [(w_key, wk), (w_value, wv), (w_query, wq), (w_out, wo), (w_conv, wc), (w_point, wp)]
        )
    ]

    def frame_load(m):
        return pltpu.make_async_copy(frames.at[m], xin.at[m, pl.ds(LC, rows)], fr_sem.at[m])

    @pl.when(first_phase)
    def _():
        for m in range(micro):
            frame_load(m).start()

    for load in loads:
        load.start()

    pl.semaphore_wait(barrier, 6)

    def sends_right(m):
        return jnp.logical_or(t < shards - 1, m < micro - 1)

    def has_left(m):
        return jnp.logical_or(t > 0, m > 0)

    def first_halo(m):
        slot = jnp.minimum(m + wrap, micro - 1)
        return pltpu.make_async_remote_copy(
            src_ref=frames.at[m, pl.ds(rows - LC, LC)],
            dst_ref=xin.at[slot, pl.ds(0, LC)],
            send_sem=xh_send.at[micro + m], recv_sem=xh_recv.at[slot],
            device_id=(t_next, p), device_id_type=MESH,
        )

    def piece_send(m, n):
        lo, hi = PIECES[n]
        return pltpu.make_async_remote_copy(
            src_ref=obuf.at[m, pl.ds(lo, hi - lo)],
            dst_ref=xin.at[m, pl.ds(LC + lo, hi - lo)],
            send_sem=x_send.at[m, n], recv_sem=x_recv.at[m, n],
            device_id=(t, p_next), device_id_type=MESH,
        )

    def to_slot(m):
        return jnp.minimum(m + wrap, micro - 1)

    def halo_send(m, slot):
        return pltpu.make_async_remote_copy(
            src_ref=obuf.at[m, pl.ds(rows - LC, LC)],
            dst_ref=xin.at[slot, pl.ds(0, LC)],
            send_sem=xh_send.at[m], recv_sem=xh_recv.at[slot],
            device_id=(t_next, p_next), device_id_type=MESH,
        )

    def mem_copy(m, slot):
        return pltpu.make_async_remote_copy(
            src_ref=mem_out.at[m], dst_ref=mem_in.at[slot],
            send_sem=mem_send.at[m], recv_sem=mem_recv.at[slot],
            device_id=(t_next, p), device_id_type=MESH,
        )

    def rim_copy(m, slot):
        return pltpu.make_async_remote_copy(
            src_ref=rim_out.at[m], dst_ref=rim_in.at[slot],
            send_sem=rim_send.at[m], recv_sem=rim_recv.at[slot],
            device_id=(t_next, p), device_id_type=MESH,
        )

    def out_copy(m):
        return pltpu.make_async_copy(obuf.at[m], out.at[0, m], out_sem.at[m])

    @pl.when(first_phase)
    def _():
        for m in range(micro):
            @pl.when(sends_right(m))
            def _():
                first_halo(m).start()

    @pl.when(t == 0)
    def _():
        xin[0, 0:LC, :] = jnp.zeros((LC, width), BF16)
        mem_in[0] = jnp.zeros(mem_in.shape[1:], BF16)
        rim_in[0] = jnp.zeros(rim_in.shape[1:], BF16)

    memk[...] = jnp.zeros(memk.shape, F32)
    memv[...] = jnp.zeros(memv.shape, F32)

    def count_of(m, rel):
        s = m * span_segs + t * segs + rel
        safe = jnp.maximum(s, 0)
        value = counts[safe // span_segs, lax.rem(safe, span_segs)]
        return jnp.where(s >= 0, value, 0)

    def one_block(m, carry):
        near = [count_of(m, rel) for rel in range(-segs, segs)]
        left = LC // SEG

        total = LC + rows

        def norm_rows(lo, hi):
            for r in range(lo, hi, 16):
                nbuf[r : r + 16, :] = layer_norm(xin[m, r : r + 16, :].astype(F32)).astype(BF16)

        @pl.when(first_phase)
        def _():
            frame_load(m).wait()

        def wait_piece(n):
            @pl.when(jnp.logical_not(first_phase))
            def _():
                piece_send(m, n).wait_recv()

        wait_piece(0)

        def sec_norm2():
            norm_rows(LC + PIECES[0][0], LC + PIECES[0][1])

        sec_norm2()

        @pl.when(has_left(m))
        def _():
            halo_send(m, m).wait_recv()

        wait_piece(1)

        def sec_norm1():
            norm_rows(0, LC)
            norm_rows(LC + PIECES[1][0], LC + PIECES[1][1])

        sec_norm1()

        @pl.when(m == 0)
        def _():
            for i in (0, 1, 2):
                loads[i].wait()

        def project(w, lhs, dst, finish):
            for n in range(width // 256):
                col = slice(n * 256, (n + 1) * 256)
                dst[:, col] = finish(dot_nn(lhs, w[:, col]))

        def plain(r):
            return r.astype(BF16)

        def scaled(r):
            return (r.astype(BF16).astype(F32) * 0.125).astype(BF16)

        nq = segs * HEADS
        hrow = lax.broadcasted_iota(jnp.int32, (HEADS, width), 0)
        hcol = lax.broadcasted_iota(jnp.int32, (HEADS, width), 1) // (width // HEADS)
        head_on = hrow == hcol

        def sec_memory():
            project(wk, nbuf[0:total, :], kbuf, plain)

            srow = lax.broadcasted_iota(jnp.int32, (16, rows), 0)
            scol = lax.broadcasted_iota(jnp.int32, (16, rows), 1)
            cnt_lane = jnp.zeros((16, rows), jnp.int32)
            cnt_col = jnp.ones((16, 1), jnp.int32)
            crow = lax.broadcasted_iota(jnp.int32, (16, 1), 0)
            for i in range(segs):
                cnt_lane = jnp.where(scol // SEG == i, near[segs + i], cnt_lane)
                cnt_col = jnp.where(crow == i, near[segs + i], cnt_col)
            pick = jnp.logical_and(srow == scol // SEG, lax.rem(scol, SEG) < cnt_lane)
            pick = jnp.where(pick, 1.0, 0.0).astype(BF16)
            summary = dot_nn(pick, nbuf[LC:total, :]) / cnt_col.astype(F32)
            nbuf[total : total + 16, :] = summary.astype(BF16)
            project(wq, nbuf[LC : total + 16, :], qbuf, scaled)

            sq = qbuf[rows : rows + 16, :].astype(F32)
            queries = jnp.concatenate(
                [
                    jnp.where(head_on, jnp.broadcast_to(sq[i : i + 1, :], (HEADS, width)), 0.0)
                    for i in range(segs)
                ],
                axis=0,
            ).astype(BF16)
            mrow = lax.broadcasted_iota(jnp.int32, (nq, total), 0) // HEADS
            mcol = lax.broadcasted_iota(jnp.int32, (nq, total), 1)
            mseg = mcol // SEG
            cnt_key = jnp.zeros((nq, total), jnp.int32)
            for i in range(left + segs):
                cnt_key = jnp.where(mseg == i, near[segs - left + i], cnt_key)
            ok = (mseg >= mrow) & (mseg <= mrow + left) & (lax.rem(mcol, SEG) < cnt_key)
            scores = jnp.where(ok, dot_nt(queries, kbuf[...]), NEG)
            project(wv, nbuf[0:total, :], vbuf, plain)
            expo = jnp.exp(scores - jnp.max(scores, axis=-1, keepdims=True))
            weights = (expo / jnp.sum(expo, axis=-1, keepdims=True)).astype(BF16)
            mixed = dot_nn(weights, vbuf[...])
            memory = jnp.concatenate(
                [
                    jnp.sum(jnp.where(head_on, mixed[i * HEADS : (i + 1) * HEADS, :], 0.0), axis=0, keepdims=True)
                    for i in range(segs)
                ]
                * 4,
                axis=0,
            ).astype(BF16)
            gbuf[0:16, :] = memory

        sec_memory()

        def sec_memproj():
            low = lax.broadcasted_iota(jnp.int32, (2 * NMEM, 256), 0) < NMEM

            def mem_project(n, c):
                col = pl.ds(pl.multiple_of(n * 256, 256), 256)
                mk = dot_nn(gbuf[0:16, :], wk[:, col])[0 : 2 * NMEM]
                mv = dot_nn(gbuf[0:16, :], wv[:, col])[0 : 2 * NMEM]
                mem_out[m, :, col] = jnp.where(low, mk, mv).astype(BF16)
                memk[0 : 2 * NMEM, col] = mk
                memv[0 : 2 * NMEM, col] = mv
                return c

            lax.fori_loop(0, width // 256, mem_project, 0, unroll=True)

        sec_memproj()

        @pl.when(sends_right(m))
        def _():
            mem_copy(m, to_slot(m)).start()

        @pl.when(m == 0)
        def _():
            for i in (3, 4, 5):
                loads[i].wait()
            for j in range(KW):
                taps[j] = jnp.broadcast_to(wc[j : j + 1, :].astype(F32), (8, width))

        quad = 4
        qw = quad * (width // HEADS)
        win = LC + SEG
        lane = lax.broadcasted_iota(jnp.int32, (1, 128), 1)
        lane_seg = lane // SEG
        biases = []
        for i in range(segs):
            cnt = jnp.zeros((1, 128), jnp.int32)
            for j in range(left + 1):
                cnt = jnp.where(lane_seg == j, near[segs - left + i + j], cnt)
            okay = (lane < win) & (lax.rem(lane, SEG) < cnt)
            for j in range(NMEM):
                okay = okay | ((lane == win + i + j) & (near[i + j] > 0))
            biases.append(jnp.where(okay, 0.0, NEG))
        qlane = lax.broadcasted_iota(jnp.int32, (1, qw), 1) // (width // HEADS)
        sel = [jnp.where(qlane == h, 1.0, 0.0).astype(BF16) for h in range(quad)]

        def attend(g):
            col = slice(g * qw, (g + 1) * qw)
            mk = memk[:, col].astype(BF16)
            mv = memv[:, col].astype(BF16)
            for i in range(segs):
                q = qbuf[i * SEG : (i + 1) * SEG, col]
                q4 = jnp.concatenate([q * sel[h] for h in range(quad)], axis=0)
                ks = jnp.concatenate([kbuf[i * SEG : i * SEG + win, col], mk], axis=0)
                vs = jnp.concatenate([vbuf[i * SEG : i * SEG + win, col], mv], axis=0)
                s = dot_nt(q4, ks) + biases[i]
                e = jnp.exp(s - jnp.max(s, axis=-1, keepdims=True))
                o = dot_nn(e.astype(BF16), vs) / jnp.sum(e, axis=-1, keepdims=True)
                ctx = jnp.where(qlane == 0, o[0:SEG], 0.0)
                for h in range(1, quad):
                    ctx = jnp.where(qlane == h, o[h * SEG : (h + 1) * SEG], ctx)
                cbuf[i * SEG : (i + 1) * SEG, col] = ctx.astype(BF16)

        def project_out(lo, hi):
            for n in range(width // 256):
                col = slice(n * 256, (n + 1) * 256)
                r = xin[m, LC + lo : LC + hi, col].astype(F32) + dot_nn(cbuf[lo:hi, :], wo[:, col])
                rbuf[lo:hi, col] = r.astype(BF16)

        vrow = lax.broadcasted_iota(jnp.int32, (rows, 1), 0)
        cnt_row = jnp.zeros((rows, 1), jnp.int32)
        for i in range(segs):
            cnt_row = jnp.where(vrow // SEG == i, near[segs + i], cnt_row)
        keep = jnp.where(lax.rem(vrow, SEG) < cnt_row, 1.0, 0.0)

        def conv_input(lo, hi):
            for r in range(lo, hi, 16):
                z = (layer_norm(rbuf[r : r + 16, :].astype(F32)) * keep[r : r + 16]).astype(BF16)
                cext[r + SEG : r + SEG + 16, :] = z.astype(F32)
                if r >= rows - SEG:
                    rim_out[m, r - rows + SEG : r - rows + SEG + 16, :] = z

        @pl.when(has_left(m))
        def _():
            mem_copy(m, m).wait_recv()

        def sec_membuf():
            low = lax.broadcasted_iota(jnp.int32, (2 * NMEM, width), 0) < NMEM
            prev = mem_in[m].astype(F32)
            memk[0 : 2 * NMEM, :] = jnp.where(low, prev, memk[0 : 2 * NMEM, :])
            memv[0 : 2 * NMEM, :] = jnp.where(low, pltpu.roll(prev, NMEM, axis=0), memv[0 : 2 * NMEM, :])

        sec_membuf()

        def sec_attend():
            for g in range(width // qw):
                attend(g)
            project_out(0, rows)
            conv_input(0, rows)

        sec_attend()

        @pl.when(sends_right(m))
        def _():
            rim_copy(m, to_slot(m)).start()

        sub = lax.broadcasted_iota(jnp.int32, (8, 128), 0)

        def conv_range(k0, k1, a0, a1, more, unroll):
            def body(cb, c):
                col = pl.ds(pl.multiple_of(cb * 128, 128), 128)
                a = {}

                def get(k):
                    if k not in a:
                        a[k] = cext[8 * k : 8 * k + 8, col]
                    return a[k]

                acc = {k: dbuf[8 * k : 8 * k + 8, col] if more else None for k in range(k0, k1)}

                def add(k, term):
                    acc[k] = term if acc[k] is None else acc[k] + term

                for s in range(8):
                    offs = [o for o in range(s, KW + 2, 8) if 2 <= o <= KW + 1]
                    prev = None
                    for k in range(k0, k1 + (1 if s else 0)):
                        y = None
                        for o in offs:
                            if a0 <= k + o // 8 < a1:
                                term = taps[o - 2, :, col] * get(k + o // 8)
                                y = term if y is None else y + term
                        if s == 0:
                            if y is not None:
                                add(k, y)
                            continue
                        if y is not None:
                            y = pltpu.roll(y, 8 - s, axis=0)
                        if k > k0 and not (prev is None and y is None):
                            head = 0.0 if prev is None else prev
                            tail = 0.0 if y is None else y
                            add(k - 1, jnp.where(sub < 8 - s, head, tail))
                        prev = y
                for k in range(k0, k1):
                    if acc[k] is not None:
                        dbuf[8 * k : 8 * k + 8, col] = acc[k]
                return c

            lax.fori_loop(0, width // 128, body, 0, unroll=unroll)

        first = SEG // 8
        every = (SEG + rows) // 8

        def gate_rows(lo, hi):
            for r in range(lo, hi, 16):
                z = layer_norm(dbuf[r : r + 16, :])
                gbuf[r : r + 16, :] = (z / (1.0 + jnp.exp(-z))).astype(BF16)

        def point_rows(lo, hi):
            def project_point(n, c):
                col = pl.ds(pl.multiple_of(n * 256, 256), 256)
                y = rbuf[lo:hi, col].astype(F32) + dot_nn(gbuf[lo:hi, :], wp[:, col])
                obuf[m, lo:hi, col] = (y * keep[lo:hi]).astype(BF16)
                return c

            lax.fori_loop(0, width // 256, project_point, 0, unroll=True)

        def finish(n):
            lo, hi = PIECES[n]
            gate_rows(lo, hi)
            point_rows(lo, hi)

        def send_piece(n):
            @pl.when(has_next)
            def _():
                piece_send(m, n).start()

        def sec_fin0():
            conv_range(PIECES[0][0] // 8, rows // 8, first, every, False, 4)
            finish(0)

        sec_fin0()

        @pl.when(has_next & sends_right(m))
        def _():
            halo_send(m, to_slot(m)).start()

        send_piece(0)


        def sec_pre():
            conv_range(0, PIECES[0][0] // 8, first, every, False, 2)

        sec_pre()

        @pl.when(has_left(m))
        def _():
            rim_copy(m, m).wait_recv()

        def sec_fin1():
            cext[0:SEG, :] = rim_in[m].astype(F32)
            conv_range(0, first, 0, first, True, 4)
            finish(1)

        sec_fin1()
        send_piece(1)
        out_copy(m).start()
        return carry

    lax.fori_loop(0, micro, one_block, 0)

    for m in range(micro):
        out_copy(m).wait()

        @pl.when(has_next)
        def _():
            for n in range(len(PIECES)):
                piece_send(m, n).wait_send()

        @pl.when(sends_right(m))
        def _():
            mem_copy(m, to_slot(m)).wait_send()
            rim_copy(m, to_slot(m)).wait_send()

            @pl.when(has_next)
            def _():
                halo_send(m, to_slot(m)).wait_send()

            @pl.when(first_phase)
            def _():
                first_halo(m).wait_send()


def per_device(frames, frame_counts, w_query, w_key, w_value, w_out, conv_kernel, w_point):
    micro, rows, width = frames.shape
    shards = lax.axis_size("tm")
    phases = lax.axis_size("phase")
    dma = pltpu.SemaphoreType.DMA
    any_spec = pl.BlockSpec(memory_space=pltpu.HBM)
    mat = pltpu.VMEM((width, width), BF16)
    return pl.pallas_call(
        functools.partial(relay_kernel, shards, phases, micro, rows, width),
        out_shape=jax.ShapeDtypeStruct((1, micro, rows, width), BF16),
        in_specs=[pl.BlockSpec(memory_space=pltpu.SMEM)] + [any_spec] * 7,
        out_specs=any_spec,
        scratch_shapes=[
            mat, mat, mat, mat, pltpu.VMEM((KW, width), BF16), mat,
            pltpu.VMEM((micro, LC + rows, width), BF16),
            pltpu.VMEM((LC + rows + 16, width), BF16),
            pltpu.VMEM((LC + rows, width), BF16),
            pltpu.VMEM((LC + rows, width), BF16),
            pltpu.VMEM((rows + 16, width), BF16),
            pltpu.VMEM((rows, width), BF16),
            pltpu.VMEM((rows, width), BF16),
            pltpu.VMEM((SEG + rows, width), F32),
            pltpu.VMEM((rows, width), F32),
            pltpu.VMEM((rows, width), BF16),
            pltpu.VMEM((micro, rows, width), BF16),
            pltpu.VMEM((KW, 8, width), F32),
            pltpu.VMEM((micro, 2 * NMEM, width), BF16),
            pltpu.VMEM((micro, 2 * NMEM, width), BF16),
            pltpu.VMEM((SEG, width), F32),
            pltpu.VMEM((SEG, width), F32),
            pltpu.VMEM((micro, SEG, width), BF16),
            pltpu.VMEM((micro, SEG, width), BF16),
            dma((6,)), dma((micro,)), dma((micro,)),
            dma((micro, len(PIECES))), dma((micro, len(PIECES))), dma((2 * micro,)), dma((micro,)),
            dma((micro,)), dma((micro,)), dma((micro,)), dma((micro,)),
        ],
        compiler_params=pltpu.CompilerParams(
            collective_id=0, has_side_effects=True, vmem_limit_bytes=54528 * 1024
        ),
    )(frame_counts, frames, w_query, w_key, w_value, w_out, conv_kernel, w_point)


def solution(mesh):
    stage = P("phase", None, None)
    return jax.shard_map(
        per_device,
        mesh=mesh,
        in_specs=(P(None, "tm", None), P(), stage, stage, stage, stage, stage, stage),
        out_specs=P("phase", None, "tm", None),
        check_vma=False,
    )
```

```python
import functools

import jax
import jax.numpy as jnp
from jax import lax
from jax.experimental import pallas as pl
from jax.experimental.pallas import tpu as pltpu
from jax.sharding import PartitionSpec as P

HEADS = 16
SEG = 32
LC = 64
NMEM = 4
KW = 31
EPS = 1e-05
NEG = -1e30
PIECES = ((64, 128), (0, 64))
F32 = jnp.float32
BF16 = jnp.bfloat16
MESH = pl.DeviceIdType.MESH


def layer_norm(v):
    width = v.shape[-1]
    c = v - jnp.sum(v, axis=-1, keepdims=True) * (1.0 / width)
    s = jnp.sum(c * c, axis=-1, keepdims=True) * (1.0 / width)
    return c * lax.rsqrt(s + EPS)


def dot_nt(a, b):
    return lax.dot_general(a, b, (((1,), (1,)), ((), ())), preferred_element_type=F32)


def dot_nn(a, b):
    return jnp.dot(a, b, preferred_element_type=F32)


def relay_kernel(
    shards, phases, micro, rows, width,
    counts, frames, w_query, w_key, w_value, w_out, w_conv, w_point,
    out,
    wq, wk, wv, wo, wc, wp,
    xin, nbuf, kbuf, vbuf, qbuf, cbuf, rbuf, cext, dbuf, gbuf, obuf, taps,
    mem_out, mem_in, memk, memv, rim_out, rim_in,
    w_sem, fr_sem, out_sem,
    x_send, x_recv, xh_send, xh_recv, mem_send, mem_recv, rim_send, rim_recv,
):
    t = lax.axis_index("tm")
    p = lax.axis_index("phase")
    segs = rows // SEG
    span_segs = shards * segs
    t_next = lax.rem(t + 1, shards)
    t_prev = lax.rem(t + shards - 1, shards)
    p_next = lax.rem(p + 1, phases)
    p_prev = lax.rem(p + phases - 1, phases)
    first_phase = p == 0
    has_next = p < phases - 1
    last_shard = t == shards - 1
    wrap = jnp.where(last_shard, 1, 0)

    barrier = pltpu.get_barrier_semaphore()
    for dt, dp in (
        (t_next, p), (t_prev, p), (t, p_next), (t, p_prev), (t_next, p_next), (t_prev, p_prev)
    ):
        pl.semaphore_signal(barrier, inc=1, device_id=(dt, dp), device_id_type=MESH)

    loads = [
        pltpu.make_async_copy(src.at[0], dst, w_sem.at[i])
        for i, (src, dst) in enumerate(
            [(w_key, wk), (w_value, wv), (w_query, wq), (w_out, wo), (w_conv, wc), (w_point, wp)]
        )
    ]

    def frame_load(m):
        return pltpu.make_async_copy(frames.at[m], xin.at[m, pl.ds(LC, rows)], fr_sem.at[m])

    @pl.when(first_phase)
    def _():
        for m in range(micro):
            frame_load(m).start()

    for load in loads:
        load.start()

    pl.semaphore_wait(barrier, 6)

    def sends_right(m):
        return jnp.logical_or(t < shards - 1, m < micro - 1)

    def has_left(m):
        return jnp.logical_or(t > 0, m > 0)

    def first_halo(m):
        slot = jnp.minimum(m + wrap, micro - 1)
        return pltpu.make_async_remote_copy(
            src_ref=frames.at[m, pl.ds(rows - LC, LC)],
            dst_ref=xin.at[slot, pl.ds(0, LC)],
            send_sem=xh_send.at[micro + m], recv_sem=xh_recv.at[slot],
            device_id=(t_next, p), device_id_type=MESH,
        )

    def piece_send(m, n):
        lo, hi = PIECES[n]
        return pltpu.make_async_remote_copy(
            src_ref=obuf.at[m, pl.ds(lo, hi - lo)],
            dst_ref=xin.at[m, pl.ds(LC + lo, hi - lo)],
            send_sem=x_send.at[m, n], recv_sem=x_recv.at[m, n],
            device_id=(t, p_next), device_id_type=MESH,
        )

    def to_slot(m):
        return jnp.minimum(m + wrap, micro - 1)

    def halo_send(m, slot):
        return pltpu.make_async_remote_copy(
            src_ref=obuf.at[m, pl.ds(rows - LC, LC)],
            dst_ref=xin.at[slot, pl.ds(0, LC)],
            send_sem=xh_send.at[m], recv_sem=xh_recv.at[slot],
            device_id=(t_next, p_next), device_id_type=MESH,
        )

    def mem_copy(m, slot):
        return pltpu.make_async_remote_copy(
            src_ref=mem_out.at[m], dst_ref=mem_in.at[slot],
            send_sem=mem_send.at[m], recv_sem=mem_recv.at[slot],
            device_id=(t_next, p), device_id_type=MESH,
        )

    def rim_copy(m, slot):
        return pltpu.make_async_remote_copy(
            src_ref=rim_out.at[m], dst_ref=rim_in.at[slot],
            send_sem=rim_send.at[m], recv_sem=rim_recv.at[slot],
            device_id=(t_next, p), device_id_type=MESH,
        )

    def out_copy(m):
        return pltpu.make_async_copy(obuf.at[m], out.at[0, m], out_sem.at[m])

    @pl.when(first_phase)
    def _():
        for m in range(micro):
            @pl.when(sends_right(m))
            def _():
                first_halo(m).start()

    @pl.when(t == 0)
    def _():
        xin[0, 0:LC, :] = jnp.zeros((LC, width), BF16)
        mem_in[0] = jnp.zeros(mem_in.shape[1:], BF16)
        rim_in[0] = jnp.zeros(rim_in.shape[1:], BF16)

    memk[...] = jnp.zeros(memk.shape, F32)
    memv[...] = jnp.zeros(memv.shape, F32)

    def count_of(m, rel):
        s = m * span_segs + t * segs + rel
        safe = jnp.maximum(s, 0)
        value = counts[safe // span_segs, lax.rem(safe, span_segs)]
        return jnp.where(s >= 0, value, 0)

    def one_block(m, carry):
        near = [count_of(m, rel) for rel in range(-segs, segs)]
        left = LC // SEG

        total = LC + rows

        def norm_rows(lo, hi):
            for r in range(lo, hi, 16):
                nbuf[r : r + 16, :] = layer_norm(xin[m, r : r + 16, :].astype(F32)).astype(BF16)

        @pl.when(first_phase)
        def _():
            frame_load(m).wait()

        def wait_piece(n):
            @pl.when(jnp.logical_not(first_phase))
            def _():
                piece_send(m, n).wait_recv()

        wait_piece(0)

        def sec_norm2():
            norm_rows(LC + PIECES[0][0], LC + PIECES[0][1])

        sec_norm2()

        @pl.when(has_left(m))
        def _():
            halo_send(m, m).wait_recv()

        wait_piece(1)

        def sec_norm1():
            norm_rows(0, LC)
            norm_rows(LC + PIECES[1][0], LC + PIECES[1][1])

        sec_norm1()

        @pl.when(m == 0)
        def _():
            for i in (0, 1, 2):
                loads[i].wait()

        def project(w, lhs, dst, finish):
            for n in range(width // 256):
                col = slice(n * 256, (n + 1) * 256)
                dst[:, col] = finish(dot_nn(lhs, w[:, col]))

        def plain(r):
            return r.astype(BF16)

        def scaled(r):
            return (r * 0.125).astype(BF16)

        nq = segs * HEADS
        hrow = lax.broadcasted_iota(jnp.int32, (HEADS, width), 0)
        hcol = lax.broadcasted_iota(jnp.int32, (HEADS, width), 1) // (width // HEADS)
        head_on = hrow == hcol

        def sec_memory():
            project(wk, nbuf[0:total, :], kbuf, plain)

            srow = lax.broadcasted_iota(jnp.int32, (16, rows), 0)
            scol = lax.broadcasted_iota(jnp.int32, (16, rows), 1)
            cnt_lane = jnp.zeros((16, rows), jnp.int32)
            cnt_col = jnp.ones((16, 1), jnp.int32)
            crow = lax.broadcasted_iota(jnp.int32, (16, 1), 0)
            for i in range(segs):
                cnt_lane = jnp.where(scol // SEG == i, near[segs + i], cnt_lane)
                cnt_col = jnp.where(crow == i, near[segs + i], cnt_col)
            pick = jnp.logical_and(srow == scol // SEG, lax.rem(scol, SEG) < cnt_lane)
            pick = jnp.where(pick, 1.0, 0.0).astype(BF16)
            summary = dot_nn(pick, nbuf[LC:total, :]) / cnt_col.astype(F32)
            nbuf[total : total + 16, :] = summary.astype(BF16)
            project(wq, nbuf[LC : total + 16, :], qbuf, scaled)

            sq = qbuf[rows : rows + 16, :].astype(F32)
            queries = jnp.concatenate(
                [
                    jnp.where(head_on, jnp.broadcast_to(sq[i : i + 1, :], (HEADS, width)), 0.0)
                    for i in range(segs)
                ],
                axis=0,
            ).astype(BF16)
            mrow = lax.broadcasted_iota(jnp.int32, (nq, total), 0) // HEADS
            mcol = lax.broadcasted_iota(jnp.int32, (nq, total), 1)
            mseg = mcol // SEG
            cnt_key = jnp.zeros((nq, total), jnp.int32)
            for i in range(left + segs):
                cnt_key = jnp.where(mseg == i, near[segs - left + i], cnt_key)
            ok = (mseg >= mrow) & (mseg <= mrow + left) & (lax.rem(mcol, SEG) < cnt_key)
            scores = jnp.where(ok, dot_nt(queries, kbuf[...]), NEG)
            project(wv, nbuf[0:total, :], vbuf, plain)
            expo = jnp.exp(scores - jnp.max(scores, axis=-1, keepdims=True))
            weights = (expo / jnp.sum(expo, axis=-1, keepdims=True)).astype(BF16)
            mixed = dot_nn(weights, vbuf[...])
            memory = jnp.concatenate(
                [
                    jnp.sum(jnp.where(head_on, mixed[i * HEADS : (i + 1) * HEADS, :], 0.0), axis=0, keepdims=True)
                    for i in range(segs)
                ]
                * 4,
                axis=0,
            ).astype(BF16)
            gbuf[0:16, :] = memory

        sec_memory()

        def sec_memproj():
            low = lax.broadcasted_iota(jnp.int32, (2 * NMEM, 256), 0) < NMEM

            def mem_project(n, c):
                col = pl.ds(pl.multiple_of(n * 256, 256), 256)
                mk = dot_nn(gbuf[0:16, :], wk[:, col])[0 : 2 * NMEM]
                mv = dot_nn(gbuf[0:16, :], wv[:, col])[0 : 2 * NMEM]
                mem_out[m, :, col] = jnp.where(low, mk, mv).astype(BF16)
                memk[0 : 2 * NMEM, col] = mk
                memv[0 : 2 * NMEM, col] = mv
                return c

            lax.fori_loop(0, width // 256, mem_project, 0, unroll=True)

        sec_memproj()

        @pl.when(sends_right(m))
        def _():
            mem_copy(m, to_slot(m)).start()

        @pl.when(m == 0)
        def _():
            for i in (3, 4, 5):
                loads[i].wait()
            for j in range(KW):
                taps[j] = jnp.broadcast_to(wc[j : j + 1, :].astype(F32), (8, width))

        quad = 4
        qw = quad * (width // HEADS)
        win = LC + SEG
        lane = lax.broadcasted_iota(jnp.int32, (1, 128), 1)
        lane_seg = lane // SEG
        biases = []
        for i in range(segs):
            cnt = jnp.zeros((1, 128), jnp.int32)
            for j in range(left + 1):
                cnt = jnp.where(lane_seg == j, near[segs - left + i + j], cnt)
            okay = (lane < win) & (lax.rem(lane, SEG) < cnt)
            for j in range(NMEM):
                okay = okay | ((lane == win + i + j) & (near[i + j] > 0))
            biases.append(jnp.where(okay, 0.0, NEG))
        qlane = lax.broadcasted_iota(jnp.int32, (1, qw), 1) // (width // HEADS)
        sel = [jnp.where(qlane == h, 1.0, 0.0).astype(BF16) for h in range(quad)]

        def attend(g):
            col = slice(g * qw, (g + 1) * qw)
            mk = memk[:, col].astype(BF16)
            mv = memv[:, col].astype(BF16)
            for i in range(segs):
                q = qbuf[i * SEG : (i + 1) * SEG, col]
                q4 = jnp.concatenate([q * sel[h] for h in range(quad)], axis=0)
                ks = jnp.concatenate([kbuf[i * SEG : i * SEG + win, col], mk], axis=0)
                vs = jnp.concatenate([vbuf[i * SEG : i * SEG + win, col], mv], axis=0)
                s = dot_nt(q4, ks) + biases[i]
                e = jnp.exp(s - jnp.max(s, axis=-1, keepdims=True))
                o = dot_nn(e.astype(BF16), vs) / jnp.sum(e, axis=-1, keepdims=True)
                ctx = jnp.where(qlane == 0, o[0:SEG], 0.0)
                for h in range(1, quad):
                    ctx = jnp.where(qlane == h, o[h * SEG : (h + 1) * SEG], ctx)
                cbuf[i * SEG : (i + 1) * SEG, col] = ctx.astype(BF16)

        def project_out(lo, hi):
            for n in range(width // 256):
                col = slice(n * 256, (n + 1) * 256)
                r = xin[m, LC + lo : LC + hi, col].astype(F32) + dot_nn(cbuf[lo:hi, :], wo[:, col])
                rbuf[lo:hi, col] = r.astype(BF16)

        vrow = lax.broadcasted_iota(jnp.int32, (rows, 1), 0)
        cnt_row = jnp.zeros((rows, 1), jnp.int32)
        for i in range(segs):
            cnt_row = jnp.where(vrow // SEG == i, near[segs + i], cnt_row)
        keep = jnp.where(lax.rem(vrow, SEG) < cnt_row, 1.0, 0.0)

        def conv_input(lo, hi):
            for r in range(lo, hi, 16):
                z = (layer_norm(rbuf[r : r + 16, :].astype(F32)) * keep[r : r + 16]).astype(BF16)
                cext[r + SEG : r + SEG + 16, :] = z.astype(F32)
                if r >= rows - SEG:
                    rim_out[m, r - rows + SEG : r - rows + SEG + 16, :] = z

        @pl.when(has_left(m))
        def _():
            mem_copy(m, m).wait_recv()

        def sec_membuf():
            low = lax.broadcasted_iota(jnp.int32, (2 * NMEM, width), 0) < NMEM
            prev = mem_in[m].astype(F32)
            memk[0 : 2 * NMEM, :] = jnp.where(low, prev, memk[0 : 2 * NMEM, :])
            memv[0 : 2 * NMEM, :] = jnp.where(low, pltpu.roll(prev, NMEM, axis=0), memv[0 : 2 * NMEM, :])

        sec_membuf()

        def sec_attend():
            for g in range(width // qw):
                attend(g)
            project_out(0, rows)
            conv_input(0, rows)

        sec_attend()

        @pl.when(sends_right(m))
        def _():
            rim_copy(m, to_slot(m)).start()

        sub = lax.broadcasted_iota(jnp.int32, (8, 128), 0)

        def conv_range(k0, k1, a0, a1, more, unroll):
            def body(cb, c):
                col = pl.ds(pl.multiple_of(cb * 128, 128), 128)
                a = {}

                def get(k):
                    if k not in a:
                        a[k] = cext[8 * k : 8 * k + 8, col]
                    return a[k]

                acc = {k: dbuf[8 * k : 8 * k + 8, col] if more else None for k in range(k0, k1)}

                def add(k, term):
                    acc[k] = term if acc[k] is None else acc[k] + term

                for s in range(8):
                    offs = [o for o in range(s, KW + 2, 8) if 2 <= o <= KW + 1]
                    prev = None
                    for k in range(k0, k1 + (1 if s else 0)):
                        y = None
                        for o in offs:
                            if a0 <= k + o // 8 < a1:
                                term = taps[o - 2, :, col] * get(k + o // 8)
                                y = term if y is None else y + term
                        if s == 0:
                            if y is not None:
                                add(k, y)
                            continue
                        if y is not None:
                            y = pltpu.roll(y, 8 - s, axis=0)
                        if k > k0 and not (prev is None and y is None):
                            head = 0.0 if prev is None else prev
                            tail = 0.0 if y is None else y
                            add(k - 1, jnp.where(sub < 8 - s, head, tail))
                        prev = y
                for k in range(k0, k1):
                    if acc[k] is not None:
                        dbuf[8 * k : 8 * k + 8, col] = acc[k]
                return c

            lax.fori_loop(0, width // 128, body, 0, unroll=unroll)

        first = SEG // 8
        every = (SEG + rows) // 8

        def gate_rows(lo, hi):
            for r in range(lo, hi, 16):
                z = layer_norm(dbuf[r : r + 16, :])
                gbuf[r : r + 16, :] = (z / (1.0 + jnp.exp(-z))).astype(BF16)

        def point_rows(lo, hi):
            def project_point(n, c):
                col = pl.ds(pl.multiple_of(n * 256, 256), 256)
                y = rbuf[lo:hi, col].astype(F32) + dot_nn(gbuf[lo:hi, :], wp[:, col])
                obuf[m, lo:hi, col] = (y * keep[lo:hi]).astype(BF16)
                return c

            lax.fori_loop(0, width // 256, project_point, 0, unroll=True)

        def finish(n):
            lo, hi = PIECES[n]
            gate_rows(lo, hi)
            point_rows(lo, hi)

        def send_piece(n):
            @pl.when(has_next)
            def _():
                piece_send(m, n).start()

        def sec_fin0():
            conv_range(PIECES[0][0] // 8, rows // 8, first, every, False, 4)
            finish(0)

        sec_fin0()

        @pl.when(has_next & sends_right(m))
        def _():
            halo_send(m, to_slot(m)).start()

        send_piece(0)


        def sec_pre():
            conv_range(0, PIECES[0][0] // 8, first, every, False, 2)

        sec_pre()

        @pl.when(has_left(m))
        def _():
            rim_copy(m, m).wait_recv()

        def sec_fin1():
            cext[0:SEG, :] = rim_in[m].astype(F32)
            conv_range(0, first, 0, first, True, 4)
            finish(1)

        sec_fin1()
        send_piece(1)
        out_copy(m).start()
        return carry

    lax.fori_loop(0, micro, one_block, 0)

    for m in range(micro):
        out_copy(m).wait()

        @pl.when(has_next)
        def _():
            for n in range(len(PIECES)):
                piece_send(m, n).wait_send()

        @pl.when(sends_right(m))
        def _():
            mem_copy(m, to_slot(m)).wait_send()
            rim_copy(m, to_slot(m)).wait_send()

            @pl.when(has_next)
            def _():
                halo_send(m, to_slot(m)).wait_send()

            @pl.when(first_phase)
            def _():
                first_halo(m).wait_send()


def per_device(frames, frame_counts, w_query, w_key, w_value, w_out, conv_kernel, w_point):
    micro, rows, width = frames.shape
    shards = lax.axis_size("tm")
    phases = lax.axis_size("phase")
    dma = pltpu.SemaphoreType.DMA
    any_spec = pl.BlockSpec(memory_space=pltpu.HBM)
    mat = pltpu.VMEM((width, width), BF16)
    return pl.pallas_call(
        functools.partial(relay_kernel, shards, phases, micro, rows, width),
        out_shape=jax.ShapeDtypeStruct((1, micro, rows, width), BF16),
        in_specs=[pl.BlockSpec(memory_space=pltpu.SMEM)] + [any_spec] * 7,
        out_specs=any_spec,
        scratch_shapes=[
            mat, mat, mat, mat, pltpu.VMEM((KW, width), BF16), mat,
            pltpu.VMEM((micro, LC + rows, width), BF16),
            pltpu.VMEM((LC + rows + 16, width), BF16),
            pltpu.VMEM((LC + rows, width), BF16),
            pltpu.VMEM((LC + rows, width), BF16),
            pltpu.VMEM((rows + 16, width), BF16),
            pltpu.VMEM((rows, width), BF16),
            pltpu.VMEM((rows, width), BF16),
            pltpu.VMEM((SEG + rows, width), F32),
            pltpu.VMEM((rows, width), F32),
            pltpu.VMEM((rows, width), BF16),
            pltpu.VMEM((micro, rows, width), BF16),
            pltpu.VMEM((KW, 8, width), F32),
            pltpu.VMEM((micro, 2 * NMEM, width), BF16),
            pltpu.VMEM((micro, 2 * NMEM, width), BF16),
            pltpu.VMEM((SEG, width), F32),
            pltpu.VMEM((SEG, width), F32),
            pltpu.VMEM((micro, SEG, width), BF16),
            pltpu.VMEM((micro, SEG, width), BF16),
            dma((6,)), dma((micro,)), dma((micro,)),
            dma((micro, len(PIECES))), dma((micro, len(PIECES))), dma((2 * micro,)), dma((micro,)),
            dma((micro,)), dma((micro,)), dma((micro,)), dma((micro,)),
        ],
        compiler_params=pltpu.CompilerParams(
            collective_id=0, has_side_effects=True, vmem_limit_bytes=54528 * 1024
        ),
    )(frame_counts, frames, w_query, w_key, w_value, w_out, conv_kernel, w_point)


def solution(mesh):
    stage = P("phase", None, None)
    return jax.shard_map(
        per_device,
        mesh=mesh,
        in_specs=(P(None, "tm", None), P(), stage, stage, stage, stage, stage, stage),
        out_specs=P("phase", None, "tm", None),
        check_vma=False,
    )
```
